512 devices in a mesh: pa: 128 (over x_lo, z, y), sa: 4 (over x_hi, core).
Axes of the slice: x: 4 (x_hi: 2, x_lo: 2; x = x_hi * 2 + x_lo), y: 4, z: 16, core: 2. Of those that a mesh axis runs over, the one named last changes fastest.
Arguments:
- raw_echo: bfloat16 [4096, 2, 32768], P('pa', None, 'sa'), may hold values from -6 to 6
- chirp_replica: bfloat16 [2, 1024], replicated, may hold values from -0.125 to 0.125
- azimuth_refs: bfloat16 [1024, 2, 512], P('pa'), may hold values from -0.1875 to 0.1875
- migration_index: int32 [4, 128], replicated, may hold values from 0 to 1023
- window_start: int32 [1], replicated, may hold values from 0 to 2047
Outputs:
- image: float32 [4, 4096, 2, 4096], P('sa', 'pa')
The draws below stay inside these ranges and needn't reach their ends.
All inputs are finite; a program needn't handle non-finite values.
Results may differ from the reference program's by a relative error of at most 0.0029.
Values may be sent and summed in bfloat16 or wider, within the bound.
A program may use at most 64 MiB of HBM per device.

```python
import math
import jax
import jax.numpy as jnp
from jax import lax

S = 32768
K = 1024
R = 16384
L = 512
RB = 256
PULSES = 4096
NREF = 1024
W = 4096
BIN_DEV = 32
AB = 256
N_PA = 128
N_SA = 4


def set_ends(entries, key, low, high):
    shape = entries.shape
    index_at = [jax.random.randint(jax.random.fold_in(key, axis), (), 0, shape[axis]) for axis in range(len(shape))]
    entries = entries.at[tuple(index_at)].set(low)
    longest = shape.index(max(shape))
    index_at[longest] = (index_at[longest] + 1) % shape[longest]
    return entries.at[tuple(index_at)].set(high)


def levels(rng, shape, split, low, largest):
    level, own = 1.0, jax.random.fold_in(rng, 6)
    for position, shards_of in split:
        draws = jnp.exp(jax.random.uniform(jax.random.fold_in(own, position), (shards_of,), jnp.float32, low / len(split), largest / len(split)))
        level = level * jnp.repeat(draws, shape[position] // shards_of).reshape([-1 if axis == position else 1 for axis in range(len(shape))])
    return level


def bell_draw(stream_key, dims, width, most, shards=(), dtype=jnp.bfloat16):
    values = jax.random.normal(stream_key, dims, jnp.float32) * width
    if len(shards) > 0:
        values = levels(stream_key, dims, shards, -0.22, 0.18) * values
    return jnp.clip(values, min=-most, max=most).astype(dtype)


def setup_inputs(seed: int = 0) -> dict:
    keys = jax.random.split(jax.random.key(seed), 6)
    return {
        "raw_echo": bell_draw(keys[0], (PULSES, 2, S), 1.0, 6.0, ((0, 128), (2, 4))),
        "chirp_replica": bell_draw(keys[1], (2, K), (2 * K) ** -0.5, 0.125),
        "azimuth_refs": bell_draw(keys[2], (NREF, 2, L), (2 * L) ** -0.5, 0.1875, ((0, 128),)),
        "migration_index": set_ends(jax.random.randint(keys[3], (N_SA, N_PA), 0, NREF), jax.random.fold_in(keys[3], 1), 0, NREF - 1).astype(jnp.int32),
        "window_start": jax.random.randint(keys[4], (1,), 0, R // (2 * N_SA)).astype(jnp.int32),
    }


def toeplitz(diagonal_taps, size):
    span_size = 2 * size - 1
    reversed_taps = diagonal_taps[..., ::-1]
    shifted = jnp.concatenate([reversed_taps[..., size - 1:], reversed_taps[..., :size - 1]], axis=-1)
    reps = (1,) * (shifted.ndim - 1) + (size,)
    tiled_flat = jnp.tile(shifted, reps)[..., : size * (span_size - 1)]
    return tiled_flat.reshape(shifted.shape[:-1] + (size, span_size - 1))[..., :size]


def tap_blocks(tap_values, size):
    block_total = tap_values.shape[1] // size + 1
    padded_taps = jnp.pad(tap_values, ((0, 0), (size, 2 * size)))
    matrices = []
    for offset_block in range(block_total):
        first_tap = offset_block * size + 1
        parts = toeplitz(padded_taps[:, first_tap:first_tap + 2 * size - 1], size)
        real_part = parts[0]
        imag_part = parts[1]
        matrices.append(jnp.stack([jnp.stack([real_part, -imag_part]), jnp.stack([imag_part, real_part])]))
    return jnp.stack(matrices)


def correlate(blocked, matrices, output_count):
    summed = jnp.zeros((blocked.shape[0], 2, output_count, blocked.shape[3]), jnp.float32)
    wide_blocks = blocked.astype(jnp.float32)
    wide_mats = matrices.astype(jnp.float32)
    for offset_block in range(matrices.shape[0]):
        piece_rows = wide_blocks[:, :, offset_block:offset_block + output_count, :]
        summed = summed + jnp.einsum("rcib,cdbn->rdin", piece_rows, wide_mats[offset_block], precision=lax.Precision.HIGHEST)
    return summed


def reference(raw_echo, chirp_replica, azimuth_refs, migration_index, window_start):
    range_mats = tap_blocks(chirp_replica, RB)
    padded = jnp.pad(raw_echo, ((0, 0), (0, 0), (0, K)))
    window = lax.dynamic_slice_in_dim(padded, window_start[0].astype(jnp.int32), R + K, 2)
    group = math.gcd(PULSES, 128)
    grouped = window.reshape(PULSES // group, group, 2, R + K)

    def compress_group(samples):
        blocked = samples.reshape(group, 2, (R + K) // RB, RB)
        focused = correlate(blocked, range_mats, R // RB)
        return focused.astype(jnp.bfloat16).reshape(group, 2, R)

    kept_bins = lax.map(compress_group, grouped).reshape(PULSES, 2, R)
    lines = jnp.transpose(kept_bins, (2, 1, 0)).reshape(N_SA * N_PA, BIN_DEV, 2, PULSES)
    flat_index = migration_index.reshape(N_SA * N_PA)

    def focus_group(inputs):
        range_lines, row_index = inputs
        reference_row = lax.dynamic_index_in_dim(azimuth_refs, row_index.astype(jnp.int32), 0, keepdims=False)
        az_mats = tap_blocks(reference_row, AB)
        block_count = PULSES // AB
        blocked = range_lines.reshape(BIN_DEV, 2, block_count, AB)
        blocked = jnp.pad(blocked, ((0, 0), (0, 0), (1, 1), (0, 0)))
        return correlate(blocked, az_mats, block_count).reshape(BIN_DEV, 2, PULSES)

    focused = lax.map(focus_group, (lines, flat_index))
    return focused.reshape(N_SA, W, 2, PULSES)
```

```python
import functools

import jax
import jax.numpy as jnp
from jax import lax
from jax.experimental import pallas as pl
from jax.experimental.pallas import tpu as pltpu
from jax.sharding import PartitionSpec as P

MESH = pl.DeviceIdType.MESH
BF16 = jnp.bfloat16
F32 = jnp.float32
NT = (((1,), (1,)), ((), ()))
SPAN = 1664
HALO = 3072
VMEM = pl.BlockSpec(memory_space=pltpu.VMEM)
SMEM = pl.BlockSpec(memory_space=pltpu.SMEM)
ANY = pl.BlockSpec(memory_space=pl.ANY)


def taps_kernel(shift_ref, chirp_ref, out_ref):
    out_ref[...] = jnp.zeros_like(out_ref)
    shift = shift_ref[0]
    for part in range(2):
        row = jnp.concatenate([chirp_ref[part : part + 1, :], jnp.zeros((1, 256), F32)], axis=1)
        row = pltpu.roll(jnp.broadcast_to(row, (8, 1280)), shift, 1)[:1]
        base = pltpu.roll(jnp.broadcast_to(row, (128, 1280)), 0, 1, stride=1, stride_axis=0)
        base = base.astype(BF16)
        for y in range(4):
            for g in range(4):
                r0 = part * 128 + g * 32
                out_ref[y, r0 : r0 + 32, 128 * g : 128 * g + 1280] = base[32 * y : 32 * y + 32, :]


def range_kernel(base_ref, w_ref, taps_ref, out_ref):
    base = base_ref[0]

    def item(t, carry):
        pieces = []
        for c in range(2):
            for x in range(2):
                off = pl.multiple_of(base + (t // 4) * 4096 + x * 2048 + (t % 4) * 512, 128)
                pieces.append(w_ref[c, :, pl.ds(off, SPAN)])
        lhs = jnp.concatenate(pieces, axis=0)
        for y in range(4):
            got = lax.dot_general(lhs, taps_ref[y], NT, preferred_element_type=F32)
            real = (got[:64, :128] + got[64:, 128:]).astype(BF16)
            imag = (got[64:, :128] - got[:64, 128:]).astype(BF16)
            for x in range(2):
                out_ref[t, x, y, 0] = real[32 * x : 32 * x + 32]
                out_ref[t, x, y, 1] = imag[32 * x : 32 * x + 32]
        return carry

    lax.fori_loop(0, 8, item, 0)


def turn_kernel(y_ref, rows_ref, turned_ref, row_ref, xr, zs, rr, rs, rz, sx, rx, sz, rz_sem, srow, rrow, szrow, rzrow):
    pa = lax.axis_index("pa")
    sa = lax.axis_index("sa")
    xlo, z, y = pa // 64, (pa // 4) % 16, pa % 4
    xhi, core = sa // 2, sa % 2
    me_plane = xlo * 4 + y

    def plane(index):
        return ((index // 4) * 16 + z) * 4 + index % 4

    def line(index):
        return (xlo * 16 + index) * 4 + y

    barrier = pltpu.get_barrier_semaphore()

    def greet_plane(i, carry):
        dev = plane(i)

        @pl.when(jnp.logical_or(dev != pa, xhi != sa))
        def _():
            pl.semaphore_signal(barrier, inc=1, device_id=(dev, xhi), device_id_type=MESH)

        return carry

    lax.fori_loop(0, 8, greet_plane, 0)

    def greet_line(i, carry):
        dev = line((z + i) % 16)
        pl.semaphore_signal(barrier, inc=1, device_id=(dev, sa), device_id_type=MESH)
        return carry

    lax.fori_loop(1, 16, greet_line, 0)

    @pl.when(sa == 0)
    def _():
        pl.semaphore_wait(barrier, 30)

    @pl.when(sa == 1)
    def _():
        pl.semaphore_wait(barrier, 31)

    @pl.when(sa >= 2)
    def _():
        pl.semaphore_wait(barrier, 15)

    @pl.when(xhi == 0)
    def _():
        def row_send(i, carry):
            jj, d = i // 8, (i + me_plane) % 8
            there = jnp.logical_or(plane(d) != pa, 2 * core + jj != sa)

            @pl.when(there)
            def _():
                pltpu.make_async_remote_copy(
                    rows_ref.at[jj, d], rr.at[me_plane], srow, rrow,
                    device_id=(plane(d), 2 * core + jj), device_id_type=MESH,
                ).start()

            @pl.when(jnp.logical_not(there))
            def _():
                pltpu.make_async_copy(rows_ref.at[jj, d], rr.at[me_plane], rrow).start()

            return carry

        lax.fori_loop(0, 16, row_send, 0)

        def send(i, carry):
            t, d = i // 8, (i + me_plane) % 8
            jj, k = t // 4, t % 4
            there = jnp.logical_or(plane(d) != pa, 2 * core + jj != sa)

            @pl.when(there)
            def _():
                pltpu.make_async_remote_copy(
                    y_ref.at[t, d], xr.at[k, :, me_plane], sx, rx.at[k],
                    device_id=(plane(d), 2 * core + jj), device_id_type=MESH,
                ).start()

            @pl.when(jnp.logical_not(there))
            def _():
                pltpu.make_async_copy(y_ref.at[t, d], xr.at[k, :, me_plane], rx.at[k]).start()

            return carry

        lax.fori_loop(0, 64, send, 0)

    eye = (
        lax.broadcasted_iota(jnp.int32, (128, 128), 0) == lax.broadcasted_iota(jnp.int32, (128, 128), 1)
    ).astype(BF16)

    pltpu.make_async_copy(rr, rr, rrow).wait()
    total = rr[0].astype(F32)
    for source in range(1, 8):
        total = total + rr[source].astype(F32)
    rs[...] = total.astype(BF16)

    def row_pass(i, carry):
        dest = (z + i) % 16
        pltpu.make_async_remote_copy(
            rs.at[dest], rz.at[z], szrow, rzrow, device_id=(line(dest), sa), device_id_type=MESH
        ).start()
        return carry

    lax.fori_loop(1, 16, row_pass, 0)
    pltpu.make_async_copy(rs.at[z], rz.at[z], rzrow).start()

    def group(k, carry):
        pltpu.make_async_copy(xr.at[k], xr.at[k], rx.at[k]).wait()
        for c in range(2):
            pulses = xr[k, c].reshape(256, 128)
            flipped = lax.dot_general(eye, pulses, NT, preferred_element_type=F32).astype(BF16)
            for g in range(4):
                for x in range(2):
                    zs[4 * k + g, c, x] = flipped[32 * g : 32 * g + 32, 128 * x : 128 * x + 128]

        def pass_on(g, inner):
            dest = 4 * k + g

            @pl.when(dest != z)
            def _():
                pltpu.make_async_remote_copy(
                    zs.at[dest], turned_ref.at[:, :, z], sz, rz_sem,
                    device_id=(line(dest), sa), device_id_type=MESH,
                ).start()

            @pl.when(dest == z)
            def _():
                pltpu.make_async_copy(zs.at[dest], turned_ref.at[:, :, z], rz_sem).start()

            return inner

        lax.fori_loop(0, 4, pass_on, 0)
        return carry

    lax.fori_loop(0, 4, group, 0)

    pltpu.make_async_copy(rz, rz, rzrow).wait()
    total = rz[0].astype(F32)
    for source in range(1, 16):
        total = total + rz[source].astype(F32)
    row_ref[...] = total.astype(BF16)

    pltpu.make_async_copy(turned_ref, turned_ref, rz_sem).wait()
    pltpu.make_async_copy(zs.at[pl.ds(0, 15)], zs.at[pl.ds(0, 15)], sz).wait()
    pltpu.make_async_copy(rs.at[pl.ds(0, 15)], rs.at[pl.ds(0, 15)], szrow).wait()

    @pl.when(xhi == 0)
    def _():
        @pl.when(core == 0)
        def _():
            for i in range(8):
                src = y_ref.at[i, pl.ds(0, 7)] if i < 4 else y_ref.at[i]
                pltpu.make_async_copy(src, src, sx).wait()
            src = rows_ref.at[0, pl.ds(0, 7)]
            pltpu.make_async_copy(src, src, srow).wait()
            src = rows_ref.at[1]
            pltpu.make_async_copy(src, src, srow).wait()

        @pl.when(core == 1)
        def _():
            pltpu.make_async_copy(y_ref, y_ref, sx).wait()
            pltpu.make_async_copy(rows_ref, rows_ref, srow).wait()


def azimuth_kernel(turned_ref, row_ref, out_ref, lhs, taps):
    zeros = jnp.zeros((32, 256), BF16)
    for c in range(2):
        lhs[c, 0] = zeros
        lhs[c, 17] = zeros
        for block in range(16):
            for half in range(2):
                tile = turned_ref[c, block // 8, 2 * (block % 8) + half]
                lhs[c, block + 1, :, 128 * half : 128 * half + 128] = tile
    for part in range(2):
        row = jnp.concatenate([row_ref[part : part + 1, :].astype(F32), jnp.zeros((1, 512), F32)], axis=1)
        wide = pltpu.roll(jnp.broadcast_to(row, (256, 1024)), 0, 1, stride=1, stride_axis=0)
        taps[256 * part : 256 * part + 256, :] = wide[:, :768].astype(BF16)
    got = []
    for c in range(2):
        total = None
        for o in range(3):
            rows = lhs[c, o : o + 16].reshape(512, 256)
            piece = lax.dot_general(rows, taps[:, 256 * o : 256 * o + 256], NT, preferred_element_type=F32)
            total = piece if total is None else total + piece
        got.append(total)
    real = got[0][:, :256] + got[1][:, 256:]
    imag = got[1][:, :256] - got[0][:, 256:]
    for block in range(16):
        out_ref[0, :, 256 * block : 256 * block + 256] = real[32 * block : 32 * block + 32]
        out_ref[1, :, 256 * block : 256 * block + 256] = imag[32 * block : 32 * block + 32]


def params(**more):
    return pltpu.CompilerParams(vmem_limit_bytes=48 << 20, **more)


def on_device(raw_echo, chirp_replica, azimuth_refs, migration_index, window_start):
    pa = lax.axis_index("pa")
    sa = lax.axis_index("sa")
    start = window_start[0]
    base = (start // 128) * 128
    taps = pl.pallas_call(
        taps_kernel,
        out_shape=jax.ShapeDtypeStruct((4, 256, SPAN), BF16),
        in_specs=[SMEM, VMEM],
        out_specs=VMEM,
        compiler_params=params(),
        name="range_taps",
    )((start - base).reshape(1), chirp_replica.astype(F32))

    planar = jnp.transpose(raw_echo, (1, 0, 2))
    halo = lax.ppermute(planar[:, :, :HALO], "sa", [(1, 0), (2, 1)])
    window = jnp.concatenate([planar, halo], axis=2)
    packed = pl.pallas_call(
        range_kernel,
        out_shape=jax.ShapeDtypeStruct((8, 2, 4, 2, 32, 128), BF16),
        in_specs=[SMEM, VMEM, VMEM],
        out_specs=VMEM,
        compiler_params=params(),
        name="range_correlate",
    )(base.reshape(1), window, taps)

    wanted = lax.dynamic_slice_in_dim(migration_index, 2 * (sa % 2), 2, 0)
    wanted = wanted.reshape(2, 2, 16, 4).transpose(0, 1, 3, 2).reshape(256)
    chosen = (wanted[:, None] == 8 * pa + jnp.arange(8)[None, :]).astype(BF16)
    rows = jnp.dot(chosen, azimuth_refs.reshape(8, 1024), preferred_element_type=F32).astype(BF16)
    rows = rows.reshape(2, 8, 16, 8, 128)

    dma = pltpu.SemaphoreType.DMA
    turned, row = pl.pallas_call(
        turn_kernel,
        out_shape=(
            jax.ShapeDtypeStruct((2, 2, 16, 32, 128), BF16),
            jax.ShapeDtypeStruct((8, 128), BF16),
        ),
        in_specs=[VMEM, VMEM],
        out_specs=(ANY, VMEM),
        scratch_shapes=[
            pltpu.VMEM((4, 2, 8, 32, 128), BF16),
            pltpu.VMEM((16, 2, 2, 32, 128), BF16),
            pltpu.VMEM((8, 16, 8, 128), BF16),
            pltpu.VMEM((16, 8, 128), BF16),
            pltpu.VMEM((16, 8, 128), BF16),
            dma, dma((4,)), dma, dma, dma, dma, dma, dma,
        ],
        compiler_params=params(collective_id=0, has_side_effects=True),
        name="corner_turn",
    )(packed.reshape(8, 8, 2, 32, 128), rows)

    image = pl.pallas_call(
        azimuth_kernel,
        out_shape=jax.ShapeDtypeStruct((2, 32, 4096), F32),
        in_specs=[VMEM, VMEM],
        out_specs=VMEM,
        scratch_shapes=[pltpu.VMEM((2, 18, 32, 256), BF16), pltpu.VMEM((512, 768), BF16)],
        compiler_params=params(),
        name="azimuth_correlate",
    )(turned, row.reshape(2, 512))
    return jnp.transpose(image, (1, 0, 2))[None]


def solution(mesh):
    placed = (P("pa", None, "sa"), P(), P("pa", None, None), P(), P())
    return jax.shard_map(
        on_device, mesh=mesh, in_specs=placed, out_specs=P("sa", "pa", None, None), check_vma=False
    )
```

```python
import functools

import jax
import jax.numpy as jnp
from jax import lax
from jax.experimental import pallas as pl
from jax.experimental.pallas import tpu as pltpu
from jax.sharding import PartitionSpec as P

MESH = pl.DeviceIdType.MESH
BF16 = jnp.bfloat16
F32 = jnp.float32
NT = (((1,), (1,)), ((), ()))
SPAN = 1664
HALO = 3072
REACH = 5248
VMEM = pl.BlockSpec(memory_space=pltpu.VMEM)
SMEM = pl.BlockSpec(memory_space=pltpu.SMEM)
ANY = pl.BlockSpec(memory_space=pl.ANY)


def prepare_kernel(start_ref, chirp_ref, planar_ref, taps_ref, window_ref, local_ref, halo_ref, tail, head):
    start = start_ref[0]
    base = pl.multiple_of((start // 128) * 128, 128)
    taps_ref[...] = jnp.zeros_like(taps_ref)
    for part in range(2):
        row = jnp.concatenate([chirp_ref[part : part + 1, :], jnp.zeros((1, 256), F32)], axis=1)
        row = pltpu.roll(jnp.broadcast_to(row, (8, 1280)), start - base, 1)[:1]
        wide = pltpu.roll(jnp.broadcast_to(row, (128, 1280)), 0, 1, stride=1, stride_axis=0)
        wide = wide.astype(BF16)
        for y in range(4):
            for g in range(4):
                r0 = part * 128 + g * 32
                taps_ref[y, r0 : r0 + 32, 128 * g : 128 * g + 1280] = wide[32 * y : 32 * y + 32, :]
    tail[:, :, :4096] = planar_ref[:, :, 4096:]
    tail[:, :, 4096:] = jnp.zeros((2, 32, HALO), BF16)
    head[:, :, :1920] = jnp.zeros((2, 32, 1920), BF16)
    head[:, :, 1920:] = planar_ref[:, :, :HALO]
    window_ref[...] = planar_ref[:, :, pl.ds(base, REACH)]
    local_ref[...] = tail[:, :, pl.ds(base, REACH)]
    halo_ref[...] = head[:, :, pl.ds(base, HALO)]


def turn_kernel(
    taps_ref, window_ref, local_ref, halo_ref, refs_ref, pick_ref, turned_ref, row_ref,
    hb, w1, yb, xr, zs, ga, rs, rz, sh, rh, sx, rx, sz, rzs, srow, rrow, szrow, rzrow,
):
    pa = lax.axis_index("pa")
    sa = lax.axis_index("sa")
    xlo, z, y = pa // 64, (pa // 4) % 16, pa % 4
    xhi, core = sa // 2, sa % 2
    here = xlo * 16 + z
    across = jnp.where(xhi == 0, xlo, 1 - xlo)
    is_source = xhi == 0

    def order(jj, t):
        return (z // 4 + t) % 4 if jj == 0 else (z // 4 + 4 - t) % 4

    barrier = pltpu.get_barrier_semaphore()

    def greet_source(i, carry):
        dev = (across * 16 + z) * 4 + i

        @pl.when(jnp.logical_or(dev != pa, xhi != sa))
        def _():
            pl.semaphore_signal(barrier, inc=1, device_id=(dev, xhi), device_id_type=MESH)

        return carry

    lax.fori_loop(0, 4, greet_source, 0)

    @pl.when(sa != 0)
    def _():
        def greet_y(i, carry):
            dev = here * 4 + (y + i) % 4
            pl.semaphore_signal(barrier, inc=1, device_id=(dev, sa), device_id_type=MESH)
            return carry

        lax.fori_loop(1, 4, greet_y, 0)

    def greet_line(i, carry):
        dev = ((here + i) % 32) * 4 + y
        pl.semaphore_signal(barrier, inc=1, device_id=(dev, sa), device_id_type=MESH)
        return carry

    lax.fori_loop(1, 32, greet_line, 0)

    @pl.when(sa < 2)
    def _():
        pl.semaphore_signal(barrier, inc=1, device_id=(pa, sa + 1), device_id_type=MESH)

    @pl.when(sa == 0)
    def _():
        pl.semaphore_wait(barrier, 38)

    @pl.when(sa == 1)
    def _():
        pl.semaphore_wait(barrier, 43)

    @pl.when(sa == 2)
    def _():
        pl.semaphore_wait(barrier, 35)

    @pl.when(sa == 3)
    def _():
        pl.semaphore_wait(barrier, 34)

    @pl.when(jnp.logical_or(sa == 1, sa == 2))
    def _():
        pltpu.make_async_remote_copy(
            halo_ref, hb, sh, rh,
            device_id=(pa, sa - 1), device_id_type=MESH,
        ).start()

    def row_send(i, carry):
        dev = here * 4 + (y + i) % 4
        pltpu.make_async_remote_copy(
            refs_ref, ga.at[y], srow, rrow, device_id=(dev, sa), device_id_type=MESH
        ).start()
        return carry

    lax.fori_loop(1, 4, row_send, 0)
    pltpu.make_async_copy(refs_ref, ga.at[y], rrow).start()

    eye = (
        lax.broadcasted_iota(jnp.int32, (128, 128), 0) == lax.broadcasted_iota(jnp.int32, (128, 128), 1)
    ).astype(BF16)

    def correlate(window, jj, k):
        pieces = []
        for c in range(2):
            for x in range(2):
                off = pl.multiple_of(x * 2048 + k * 512, 128)
                pieces.append(window[c, :, pl.ds(off, SPAN)])
        lhs = jnp.concatenate(pieces, axis=0)
        for dest in range(4):
            got = lax.dot_general(lhs, taps_ref[dest], NT, preferred_element_type=F32)
            real = (got[:64, :128] + got[64:, 128:]).astype(BF16)
            imag = (got[64:, :128] - got[:64, 128:]).astype(BF16)
            slot = (jj * 4 + k) * 4 + dest
            for x in range(2):
                yb[slot, x, 0] = real[32 * x : 32 * x + 32]
                yb[slot, x, 1] = imag[32 * x : 32 * x + 32]

        def send(i, carry):
            dest = (y + i) % 4
            dev = ((jnp.where(core == 0, xlo, 1 - xlo)) * 16 + z) * 4 + dest
            target = 2 * core + jj
            there = jnp.logical_or(dev != pa, target != sa)
            slot = (jj * 4 + k) * 4 + dest

            @pl.when(there)
            def _():
                pltpu.make_async_remote_copy(
                    yb.at[slot], xr.at[k, :, :, y], sx, rx.at[k],
                    device_id=(dev, target), device_id_type=MESH,
                ).start()

            @pl.when(jnp.logical_not(there))
            def _():
                pltpu.make_async_copy(yb.at[slot], xr.at[k, :, :, y], rx.at[k]).start()

            return carry

        lax.fori_loop(0, 4, send, 0)

    def pass_on(k):
        pltpu.make_async_copy(xr.at[k], xr.at[k], rx.at[k]).wait()
        for x in range(2):
            pulses = xr[k, x].reshape(256, 128)
            flipped = lax.dot_general(eye, pulses, NT, preferred_element_type=F32).astype(BF16)
            for g in range(4):
                for c in range(2):
                    zs[16 * x + 4 * k + g, c] = flipped[32 * g : 32 * g + 32, 128 * c : 128 * c + 128]

        def send(i, carry):
            dest = (i // 4) * 16 + 4 * k + i % 4

            @pl.when(dest != here)
            def _():
                pltpu.make_async_remote_copy(
                    zs.at[dest], turned_ref.at[:, across * 16 + z], sz, rzs,
                    device_id=(dest * 4 + y, sa), device_id_type=MESH,
                ).start()

            @pl.when(dest == here)
            def _():
                pltpu.make_async_copy(zs.at[dest], turned_ref.at[:, across * 16 + z], rzs).start()

            return carry

        lax.fori_loop(0, 8, send, 0)

    @pl.when(is_source)
    def _():
        def first(t, carry):
            correlate(window_ref, 0, order(0, t))

            @pl.when(jnp.logical_and(sa == 0, t >= 1))
            def _():
                pass_on(order(0, t - 1))

            return carry

        lax.fori_loop(0, 4, first, 0)
        pltpu.make_async_copy(hb, hb, rh).wait()
        w1[:, :, : REACH - HALO] = local_ref[:, :, : REACH - HALO]
        w1[:, :, REACH - HALO :] = local_ref[:, :, REACH - HALO :] + hb[...]

    pltpu.make_async_copy(ga, ga, rrow).wait()
    wanted = jnp.dot(pick_ref[...], ga[...].reshape(64, 512), preferred_element_type=F32)
    for dest in range(32):
        rs[dest] = wanted[2 * dest : 2 * dest + 2]

    def row_pass(i, carry):
        dest = (here + i) % 32
        pltpu.make_async_remote_copy(
            rs.at[dest], rz.at[here], szrow, rzrow, device_id=(dest * 4 + y, sa), device_id_type=MESH
        ).start()
        return carry

    lax.fori_loop(1, 32, row_pass, 0)
    pltpu.make_async_copy(rs.at[here], rz.at[here], rzrow).start()

    @pl.when(is_source)
    def _():
        def second(t, carry):
            correlate(w1, 1, order(1, t))

            @pl.when(jnp.logical_or(jnp.logical_and(sa == 0, t == 0), jnp.logical_and(sa == 1, t >= 1)))
            def _():
                pass_on(jnp.where(sa == 0, order(0, 3), order(1, t - 1)))

            return carry

        lax.fori_loop(0, 4, second, 0)

    def rest(t, carry):
        pass_on(jnp.where(core == 0, order(0, t), order(1, t)))
        return carry

    lax.fori_loop(jnp.where(sa == 0, 4, jnp.where(sa == 1, 3, 0)), 4, rest, 0)

    pltpu.make_async_copy(rz, rz, rzrow).wait()
    row_ref[...] = jnp.sum(rz[...], axis=0)

    pltpu.make_async_copy(turned_ref, turned_ref, rzs).wait()
    pltpu.make_async_copy(zs.at[pl.ds(0, 31)], zs.at[pl.ds(0, 31)], sz).wait()
    pltpu.make_async_copy(rs.at[pl.ds(0, 31)], rs.at[pl.ds(0, 31)], szrow).wait()
    pltpu.make_async_copy(ga.at[pl.ds(0, 3)], ga.at[pl.ds(0, 3)], srow).wait()

    @pl.when(jnp.logical_or(sa == 1, sa == 2))
    def _():
        pltpu.make_async_copy(halo_ref, halo_ref, sh).wait()

    @pl.when(sa == 0)
    def _():
        pltpu.make_async_copy(yb.at[pl.ds(0, 28)], yb.at[pl.ds(0, 28)], sx).wait()

    @pl.when(sa == 1)
    def _():
        pltpu.make_async_copy(yb, yb, sx).wait()


def azimuth_kernel(turned_ref, row_ref, out_ref, lhs, taps):
    zeros = jnp.zeros((32, 256), BF16)
    for c in range(2):
        lhs[c, 0] = zeros
        lhs[c, 17] = zeros
        for block in range(16):
            for half in range(2):
                tile = turned_ref[c, 2 * block + half]
                lhs[c, block + 1, :, 128 * half : 128 * half + 128] = tile
    for part in range(2):
        row = jnp.concatenate([row_ref[part : part + 1, :], jnp.zeros((1, 512), F32)], axis=1)
        wide = pltpu.roll(jnp.broadcast_to(row, (256, 1024)), 0, 1, stride=1, stride_axis=0)
        taps[256 * part : 256 * part + 256, :] = wide[:, :768].astype(BF16)
    got = []
    for c in range(2):
        total = None
        for o in range(3):
            rows = lhs[c, o : o + 16].reshape(512, 256)
            piece = lax.dot_general(rows, taps[:, 256 * o : 256 * o + 256], NT, preferred_element_type=F32)
            total = piece if total is None else total + piece
        got.append(total)
    real = got[0][:, :256] + got[1][:, 256:]
    imag = got[1][:, :256] - got[0][:, 256:]
    for block in range(16):
        out_ref[0, :, 256 * block : 256 * block + 256] = real[32 * block : 32 * block + 32]
        out_ref[1, :, 256 * block : 256 * block + 256] = imag[32 * block : 32 * block + 32]


def params(**more):
    return pltpu.CompilerParams(vmem_limit_bytes=48 << 20, **more)


def on_device(raw_echo, chirp_replica, azimuth_refs, migration_index, window_start):
    pa = lax.axis_index("pa")
    sa = lax.axis_index("sa")
    planar = jnp.transpose(raw_echo, (1, 0, 2))
    taps, window, local, halo = pl.pallas_call(
        prepare_kernel,
        out_shape=(
            jax.ShapeDtypeStruct((4, 256, SPAN), BF16),
            jax.ShapeDtypeStruct((2, 32, REACH), BF16),
            jax.ShapeDtypeStruct((2, 32, REACH), BF16),
            jax.ShapeDtypeStruct((2, 32, HALO), BF16),
        ),
        in_specs=[SMEM, VMEM, VMEM],
        out_specs=(VMEM,) * 4,
        scratch_shapes=[pltpu.VMEM((2, 32, 7168), BF16), pltpu.VMEM((2, 32, 4992), BF16)],
        compiler_params=params(),
        name="prepare",
    )(window_start, chirp_replica.astype(F32), planar)

    index = lax.dynamic_slice_in_dim(migration_index, sa, 1, 0).reshape(32, 4)
    index = lax.dynamic_slice_in_dim(index, pa % 4, 1, 1)[:, :, None]
    slot = 2 * (index % 32) + jnp.arange(2)[None, :, None]
    picked = jnp.logical_and(index // 32 == pa // 4, slot == jnp.arange(64)[None, None, :])
    pick = picked.reshape(64, 64).astype(BF16)

    dma = pltpu.SemaphoreType.DMA
    turned, row = pl.pallas_call(
        turn_kernel,
        out_shape=(
            jax.ShapeDtypeStruct((2, 32, 32, 128), BF16),
            jax.ShapeDtypeStruct((2, 512), F32),
        ),
        in_specs=[VMEM] * 6,
        out_specs=(ANY, VMEM),
        scratch_shapes=[
            pltpu.VMEM((2, 32, HALO), BF16),
            pltpu.VMEM((2, 32, REACH), BF16),
            pltpu.VMEM((32, 2, 2, 32, 128), BF16),
            pltpu.VMEM((4, 2, 2, 4, 32, 128), BF16),
            pltpu.VMEM((32, 2, 32, 128), BF16),
            pltpu.VMEM((4, 16, 512), BF16),
            pltpu.VMEM((32, 2, 512), F32),
            pltpu.VMEM((32, 2, 512), F32),
            dma, dma, dma, dma((4,)), dma, dma, dma, dma, dma, dma,
        ],
        compiler_params=params(collective_id=0, has_side_effects=True),
        name="corner_turn",
    )(taps, window, local, halo, azimuth_refs.reshape(16, 512), pick)

    image = pl.pallas_call(
        azimuth_kernel,
        out_shape=jax.ShapeDtypeStruct((2, 32, 4096), F32),
        in_specs=[VMEM, VMEM],
        out_specs=VMEM,
        scratch_shapes=[pltpu.VMEM((2, 18, 32, 256), BF16), pltpu.VMEM((512, 768), BF16)],
        compiler_params=params(),
        name="azimuth_correlate",
    )(turned, row)
    return jnp.transpose(image, (1, 0, 2))[None]


def solution(mesh):
    placed = (P("pa", None, "sa"), P(), P("pa", None, None), P(), P())
    return jax.shard_map(
        on_device, mesh=mesh, in_specs=placed, out_specs=P("sa", "pa", None, None), check_vma=False
    )
```

```python
import functools

import jax
import jax.numpy as jnp
from jax import lax
from jax.experimental import pallas as pl
from jax.experimental.pallas import tpu as pltpu
from jax.sharding import PartitionSpec as P

MESH = pl.DeviceIdType.MESH
BF16 = jnp.bfloat16
F32 = jnp.float32
NT = (((1,), (1,)), ((), ()))
SPAN = 1664
HALO = 3072
REACH = 5248
VMEM = pl.BlockSpec(memory_space=pltpu.VMEM)
SMEM = pl.BlockSpec(memory_space=pltpu.SMEM)
ANY = pl.BlockSpec(memory_space=pl.ANY)


def prepare_kernel(
    start_ref, index_ref, chirp_ref, planar_ref, taps_ref, window_ref, local_ref, halo_ref, pick_ref, tail, head
):
    pa = lax.axis_index("pa")
    sa = lax.axis_index("sa")
    line = lax.broadcasted_iota(jnp.int32, (64, 64), 0)
    code = jnp.full((64, 64), -2, jnp.int32)
    for dest in range(32):
        index = index_ref[sa, 4 * dest + pa % 4]
        code = jnp.where(line // 2 == dest, jnp.where(index // 32 == pa // 4, 2 * (index % 32), -2), code)
    pick_ref[...] = (lax.broadcasted_iota(jnp.int32, (64, 64), 1) == code + line % 2).astype(F32).astype(BF16)

    start = start_ref[0]
    base = pl.multiple_of((start // 128) * 128, 128)
    taps_ref[...] = jnp.zeros_like(taps_ref)
    for part in range(2):
        row = jnp.concatenate([chirp_ref[part : part + 1, :].astype(F32), jnp.zeros((1, 256), F32)], axis=1)
        row = pltpu.roll(jnp.broadcast_to(row, (8, 1280)), start - base, 1)[:1]
        wide = pltpu.roll(jnp.broadcast_to(row, (128, 1280)), 0, 1, stride=1, stride_axis=0)
        wide = wide.astype(BF16)
        for y in range(4):
            for g in range(4):
                r0 = part * 128 + g * 32
                taps_ref[y, r0 : r0 + 32, 128 * g : 128 * g + 1280] = wide[32 * y : 32 * y + 32, :]
    tail[:, :, :4096] = planar_ref[:, :, 4096:]
    tail[:, :, 4096:] = jnp.zeros((2, 32, HALO), BF16)
    head[:, :, :1920] = jnp.zeros((2, 32, 1920), BF16)
    head[:, :, 1920:] = planar_ref[:, :, :HALO]
    window_ref[...] = planar_ref[:, :, pl.ds(base, REACH)]
    local_ref[...] = tail[:, :, pl.ds(base, REACH)]
    halo_ref[...] = head[:, :, pl.ds(base, HALO)]


def turn_kernel(
    taps_ref, window_ref, local_ref, halo_ref, refs_ref, pick_ref, turned_ref, row_ref,
    hb, w1, yb, xr, zs, ga, rs, rz, sh, rh, sx, rx, sz, rzs, srow, rrow, szrow, rzrow,
):
    pa = lax.axis_index("pa")
    sa = lax.axis_index("sa")
    xlo, z, y = pa // 64, (pa // 4) % 16, pa % 4
    xhi, core = sa // 2, sa % 2
    here = xlo * 16 + z
    across = jnp.where(xhi == 0, xlo, 1 - xlo)
    is_source = xhi == 0

    barrier = pltpu.get_barrier_semaphore()

    def greet_source(i, carry):
        dev = (across * 16 + z) * 4 + i

        @pl.when(jnp.logical_or(dev != pa, xhi != sa))
        def _():
            pl.semaphore_signal(barrier, inc=1, device_id=(dev, xhi), device_id_type=MESH)

        return carry

    lax.fori_loop(0, 4, greet_source, 0)

    @pl.when(sa != 0)
    def _():
        def greet_y(i, carry):
            dev = here * 4 + (y + i) % 4
            pl.semaphore_signal(barrier, inc=1, device_id=(dev, sa), device_id_type=MESH)
            return carry

        lax.fori_loop(1, 4, greet_y, 0)

    def greet_line(i, carry):
        dev = ((here + i) % 32) * 4 + y
        pl.semaphore_signal(barrier, inc=1, device_id=(dev, sa), device_id_type=MESH)
        return carry

    lax.fori_loop(1, 32, greet_line, 0)

    @pl.when(sa < 2)
    def _():
        pl.semaphore_signal(barrier, inc=1, device_id=(pa, sa + 1), device_id_type=MESH)

    @pl.when(sa == 0)
    def _():
        pl.semaphore_wait(barrier, 38)

    @pl.when(sa == 1)
    def _():
        pl.semaphore_wait(barrier, 43)

    @pl.when(sa == 2)
    def _():
        pl.semaphore_wait(barrier, 35)

    @pl.when(sa == 3)
    def _():
        pl.semaphore_wait(barrier, 34)

    @pl.when(jnp.logical_or(sa == 1, sa == 2))
    def _():
        pltpu.make_async_remote_copy(
            halo_ref, hb, sh, rh,
            device_id=(pa, sa - 1), device_id_type=MESH,
        ).start()

    def row_send(i, carry):
        dev = here * 4 + (y + i) % 4
        pltpu.make_async_remote_copy(
            refs_ref, ga.at[y], srow, rrow, device_id=(dev, sa), device_id_type=MESH
        ).start()
        return carry

    lax.fori_loop(1, 4, row_send, 0)
    pltpu.make_async_copy(refs_ref, ga.at[y], rrow).start()

    eye = (
        lax.broadcasted_iota(jnp.int32, (128, 128), 0) == lax.broadcasted_iota(jnp.int32, (128, 128), 1)
    ).astype(BF16)

    def correlate(window, jj, t):
        first = (z // 4 + t) % 2
        pieces = []
        for c in range(2):
            for kk in range(2):
                for x in range(2):
                    off = pl.multiple_of(x * 2048 + (first + 2 * kk) * 512, 128)
                    pieces.append(window[c, :, pl.ds(off, SPAN)])
        lhs = jnp.concatenate(pieces, axis=0)
        for dest in range(4):
            got = lax.dot_general(lhs, taps_ref[dest], NT, preferred_element_type=F32)
            real = (got[:128, :128] + got[128:, 128:]).astype(BF16)
            imag = (got[128:, :128] - got[:128, 128:]).astype(BF16)
            for kk in range(2):
                slot = (jj * 4 + first + 2 * kk) * 4 + dest
                for x in range(2):
                    r0 = 64 * kk + 32 * x
                    yb[slot, x, 0] = real[r0 : r0 + 32]
                    yb[slot, x, 1] = imag[r0 : r0 + 32]

        def send(i, carry):
            k, dest = first + 2 * (i // 4), (y + i) % 4
            dev = ((jnp.where(core == 0, xlo, 1 - xlo)) * 16 + z) * 4 + dest
            target = 2 * core + jj
            there = jnp.logical_or(dev != pa, target != sa)
            slot = (jj * 4 + k) * 4 + dest

            @pl.when(there)
            def _():
                pltpu.make_async_remote_copy(
                    yb.at[slot], xr.at[k, :, :, y], sx, rx.at[k],
                    device_id=(dev, target), device_id_type=MESH,
                ).start()

            @pl.when(jnp.logical_not(there))
            def _():
                pltpu.make_async_copy(yb.at[slot], xr.at[k, :, :, y], rx.at[k]).start()

            return carry

        lax.fori_loop(0, 8, send, 0)

    def pass_on(k):
        pltpu.make_async_copy(xr.at[k], xr.at[k], rx.at[k]).wait()
        for x in range(2):
            pulses = xr[k, x].reshape(256, 128)
            flipped = lax.dot_general(eye, pulses, NT, preferred_element_type=F32).astype(BF16)
            for g in range(4):
                for c in range(2):
                    zs[16 * x + 4 * k + g, c] = flipped[32 * g : 32 * g + 32, 128 * c : 128 * c + 128]

        def send(i, carry):
            dest = (i // 4) * 16 + 4 * k + i % 4

            @pl.when(dest != here)
            def _():
                pltpu.make_async_remote_copy(
                    zs.at[dest], turned_ref.at[:, across * 16 + z], sz, rzs,
                    device_id=(dest * 4 + y, sa), device_id_type=MESH,
                ).start()

            @pl.when(dest == here)
            def _():
                pltpu.make_async_copy(zs.at[dest], turned_ref.at[:, across * 16 + z], rzs).start()

            return carry

        lax.fori_loop(0, 8, send, 0)

    @pl.when(is_source)
    def _():
        def first_half(t, carry):
            correlate(window_ref, 0, t)
            return carry

        lax.fori_loop(0, 2, first_half, 0)
        pltpu.make_async_copy(hb, hb, rh).wait()
        w1[:, :, : REACH - HALO] = local_ref[:, :, : REACH - HALO]
        w1[:, :, REACH - HALO :] = local_ref[:, :, REACH - HALO :] + hb[...]

        def second_half(t, carry):
            correlate(w1, 1, t)
            return carry

        lax.fori_loop(0, 2, second_half, 0)

    pltpu.make_async_copy(ga, ga, rrow).wait()
    wanted = jnp.dot(pick_ref[...], ga[...].reshape(64, 512), preferred_element_type=F32)
    for dest in range(32):
        rs[dest] = wanted[2 * dest : 2 * dest + 2]

    def row_pass(i, carry):
        dest = (here + i) % 32
        pltpu.make_async_remote_copy(
            rs.at[dest], rz.at[here], szrow, rzrow, device_id=(dest * 4 + y, sa), device_id_type=MESH
        ).start()
        return carry

    lax.fori_loop(1, 32, row_pass, 0)
    pltpu.make_async_copy(rs.at[here], rz.at[here], rzrow).start()

    def rest(t, carry):
        pass_on((z // 4 + t // 2) % 2 + 2 * (t % 2))
        return carry

    lax.fori_loop(0, 4, rest, 0)

    pltpu.make_async_copy(rz, rz, rzrow).wait()
    row_ref[...] = jnp.sum(rz[...], axis=0)

    pltpu.make_async_copy(turned_ref, turned_ref, rzs).wait()
    pltpu.make_async_copy(zs.at[pl.ds(0, 31)], zs.at[pl.ds(0, 31)], sz).wait()
    pltpu.make_async_copy(rs.at[pl.ds(0, 31)], rs.at[pl.ds(0, 31)], szrow).wait()
    pltpu.make_async_copy(ga.at[pl.ds(0, 3)], ga.at[pl.ds(0, 3)], srow).wait()

    @pl.when(jnp.logical_or(sa == 1, sa == 2))
    def _():
        pltpu.make_async_copy(halo_ref, halo_ref, sh).wait()

    @pl.when(sa == 0)
    def _():
        pltpu.make_async_copy(yb.at[pl.ds(0, 28)], yb.at[pl.ds(0, 28)], sx).wait()

    @pl.when(sa == 1)
    def _():
        pltpu.make_async_copy(yb, yb, sx).wait()


def azimuth_kernel(turned_ref, row_ref, out_ref, lhs, taps):
    zeros = jnp.zeros((32, 256), BF16)
    for c in range(2):
        lhs[c, 0] = zeros
        lhs[c, 17] = zeros
        for block in range(16):
            for half in range(2):
                tile = turned_ref[c, 2 * block + half]
                lhs[c, block + 1, :, 128 * half : 128 * half + 128] = tile
    for part in range(2):
        row = jnp.concatenate([row_ref[part : part + 1, :], jnp.zeros((1, 512), F32)], axis=1)
        wide = pltpu.roll(jnp.broadcast_to(row, (256, 1024)), 0, 1, stride=1, stride_axis=0)
        taps[256 * part : 256 * part + 256, :] = wide[:, :768].astype(BF16)
    got = []
    for c in range(2):
        total = None
        for o in range(3):
            rows = lhs[c, o : o + 16].reshape(512, 256)
            piece = lax.dot_general(rows, taps[:, 256 * o : 256 * o + 256], NT, preferred_element_type=F32)
            total = piece if total is None else total + piece
        got.append(total)
    real = got[0][:, :256] + got[1][:, 256:]
    imag = got[1][:, :256] - got[0][:, 256:]
    for block in range(16):
        out_ref[0, :, 256 * block : 256 * block + 256] = real[32 * block : 32 * block + 32]
        out_ref[1, :, 256 * block : 256 * block + 256] = imag[32 * block : 32 * block + 32]


def params(**more):
    return pltpu.CompilerParams(vmem_limit_bytes=20 << 20, **more)


def on_device(raw_echo, chirp_replica, azimuth_refs, migration_index, window_start):
    planar = jnp.transpose(raw_echo, (1, 0, 2))
    taps, window, local, halo, pick = pl.pallas_call(
        prepare_kernel,
        out_shape=(
            jax.ShapeDtypeStruct((4, 256, SPAN), BF16),
            jax.ShapeDtypeStruct((2, 32, REACH), BF16),
            jax.ShapeDtypeStruct((2, 32, REACH), BF16),
            jax.ShapeDtypeStruct((2, 32, HALO), BF16),
            jax.ShapeDtypeStruct((64, 64), BF16),
        ),
        in_specs=[SMEM, SMEM, VMEM, VMEM],
        out_specs=(VMEM,) * 5,
        scratch_shapes=[pltpu.VMEM((2, 32, 7168), BF16), pltpu.VMEM((2, 32, 4992), BF16)],
        compiler_params=params(),
        name="prepare",
    )(window_start, migration_index, chirp_replica, planar)

    dma = pltpu.SemaphoreType.DMA
    turned, row = pl.pallas_call(
        turn_kernel,
        out_shape=(
            jax.ShapeDtypeStruct((2, 32, 32, 128), BF16),
            jax.ShapeDtypeStruct((2, 512), F32),
        ),
        in_specs=[VMEM] * 6,
        out_specs=(ANY, VMEM),
        scratch_shapes=[
            pltpu.VMEM((2, 32, HALO), BF16),
            pltpu.VMEM((2, 32, REACH), BF16),
            pltpu.VMEM((32, 2, 2, 32, 128), BF16),
            pltpu.VMEM((4, 2, 2, 4, 32, 128), BF16),
            pltpu.VMEM((32, 2, 32, 128), BF16),
            pltpu.VMEM((4, 8, 2, 512), BF16),
            pltpu.VMEM((32, 2, 512), F32),
            pltpu.VMEM((32, 2, 512), F32),
            dma, dma, dma, dma((4,)), dma, dma, dma, dma, dma, dma,
        ],
        compiler_params=params(collective_id=0, has_side_effects=True),
        name="corner_turn",
    )(taps, window, local, halo, azimuth_refs, pick)

    image = pl.pallas_call(
        azimuth_kernel,
        out_shape=jax.ShapeDtypeStruct((2, 32, 4096), F32),
        in_specs=[VMEM, VMEM],
        out_specs=VMEM,
        scratch_shapes=[pltpu.VMEM((2, 18, 32, 256), BF16), pltpu.VMEM((512, 768), BF16)],
        compiler_params=params(),
        name="azimuth_correlate",
    )(turned, row)
    return jnp.transpose(image, (1, 0, 2))[None]


def solution(mesh):
    placed = (P("pa", None, "sa"), P(), P("pa", None, None), P(), P())
    return jax.shard_map(
        on_device, mesh=mesh, in_specs=placed, out_specs=P("sa", "pa", None, None), check_vma=False
    )
```

```python
import functools

import jax
import jax.numpy as jnp
from jax import lax
from jax.experimental import pallas as pl
from jax.experimental.pallas import tpu as pltpu
from jax.sharding import PartitionSpec as P

MESH = pl.DeviceIdType.MESH
BF16 = jnp.bfloat16
F32 = jnp.float32
NT = (((1,), (1,)), ((), ()))
SPAN = 1664
HALO = 3072
REACH = 5248
VMEM = pl.BlockSpec(memory_space=pltpu.VMEM)
SMEM = pl.BlockSpec(memory_space=pltpu.SMEM)
ANY = pl.BlockSpec(memory_space=pl.ANY)


def turn_kernel(
    start_ref, index_hbm, chirp_hbm, planar_ref, refs_ref, turned_ref, row_ref,
    index_ref, chirp_ref, taps_ref, pick_ref, w0, w1, halo_ref, hb, yb, xr, zs, ga, rs, rz, sin, sh, rh, sx, rx, sz, rzs, srow, rrow, szrow, rzrow,
):
    pa = lax.axis_index("pa")
    sa = lax.axis_index("sa")
    xlo, z, y = pa // 64, (pa // 4) % 16, pa % 4
    xhi, core = sa // 2, sa % 2
    here = xlo * 16 + z
    across = jnp.where(xhi == 0, xlo, 1 - xlo)
    is_source = xhi == 0

    get_index = pltpu.make_async_copy(index_hbm, index_ref, sin.at[0])
    get_chirp = pltpu.make_async_copy(chirp_hbm, chirp_ref, sin.at[1])
    get_index.start()
    get_chirp.start()

    barrier = pltpu.get_barrier_semaphore()

    def greet_source(i, carry):
        dev = (across * 16 + z) * 4 + i

        @pl.when(jnp.logical_or(dev != pa, xhi != sa))
        def _():
            pl.semaphore_signal(barrier, inc=1, device_id=(dev, xhi), device_id_type=MESH)

        return carry

    lax.fori_loop(0, 4, greet_source, 0)

    @pl.when(sa != 0)
    def _():
        def greet_y(i, carry):
            dev = here * 4 + (y + i) % 4
            pl.semaphore_signal(barrier, inc=1, device_id=(dev, sa), device_id_type=MESH)
            return carry

        lax.fori_loop(1, 4, greet_y, 0)

    def greet_line(i, carry):
        dev = ((here + i) % 32) * 4 + y
        pl.semaphore_signal(barrier, inc=1, device_id=(dev, sa), device_id_type=MESH)
        return carry

    lax.fori_loop(1, 32, greet_line, 0)

    @pl.when(sa < 2)
    def _():
        pl.semaphore_signal(barrier, inc=1, device_id=(pa, sa + 1), device_id_type=MESH)

    start = start_ref[0]
    bits = [jnp.bitwise_and(lax.shift_right_logical(start, bit), 1) == 1 for bit in range(11)]

    def shifted(value):
        for bit in (10, 9, 8, 7):
            step = 1 << bit
            value = jnp.where(bits[bit], value[:, step:], value[:, : value.shape[1] - step])
        return value

    get_chirp.wait()

    @pl.when(is_source)
    def _():
        for part in range(2):
            row = jnp.concatenate([chirp_ref[part : part + 1, :].astype(F32), jnp.zeros((1, 256), F32)], axis=1)
            row = jnp.broadcast_to(row, (8, 1280))
            for bit in range(7):
                row = jnp.where(bits[bit], pltpu.roll(row, 1 << bit, 1), row)
            wide = pltpu.roll(jnp.broadcast_to(row[:1], (128, 1280)), 0, 1, stride=1, stride_axis=0)
            wide = wide.astype(BF16)
            for dest in range(4):
                for g in range(4):
                    r0 = part * 128 + g * 32
                    if g > 0:
                        taps_ref[dest, r0 : r0 + 32, : 128 * g] = jnp.zeros((32, 128 * g), BF16)
                    taps_ref[dest, r0 : r0 + 32, 128 * g : 128 * g + 1280] = wide[32 * dest : 32 * dest + 32, :]
                    if g < 3:
                        taps_ref[dest, r0 : r0 + 32, 128 * g + 1280 :] = jnp.zeros((32, 384 - 128 * g), BF16)
        for c in range(2):
            for r0 in (0, 16):
                w0[c, r0 : r0 + 16, :] = shifted(planar_ref[c, r0 : r0 + 16, :7168])

    @pl.when(jnp.logical_or(sa == 1, sa == 2))
    def _():
        for c in range(2):
            for r0 in (0, 16):
                head = jnp.concatenate([jnp.zeros((16, 1920), BF16), planar_ref[c, r0 : r0 + 16, :HALO]], axis=1)
                halo_ref[c, r0 : r0 + 16, :] = shifted(head)

    get_index.wait()
    entry = lax.broadcasted_iota(jnp.int32, (64, 64), 0)
    code = jnp.full((64, 64), -2, jnp.int32)
    for dest in range(32):
        index = index_ref[sa, 4 * dest + y]
        code = jnp.where(entry // 2 == dest, jnp.where(index // 32 == pa // 4, 2 * (index % 32), -2), code)
    pick_ref[...] = (lax.broadcasted_iota(jnp.int32, (64, 64), 1) == code + entry % 2).astype(F32).astype(BF16)

    def correlate(window, jj, t):
        first = (z // 4 + t) % 2
        pieces = []
        for c in range(2):
            for kk in range(2):
                for x in range(2):
                    off = pl.multiple_of(x * 2048 + (first + 2 * kk) * 512, 128)
                    pieces.append(window[c, :, pl.ds(off, SPAN)])
        lhs = jnp.concatenate(pieces, axis=0)
        for dest in range(4):
            got = lax.dot_general(lhs, taps_ref[dest], NT, preferred_element_type=F32)
            real = (got[:128, :128] + got[128:, 128:]).astype(BF16)
            imag = (got[128:, :128] - got[:128, 128:]).astype(BF16)
            for kk in range(2):
                slot = (jj * 4 + first + 2 * kk) * 4 + dest
                for x in range(2):
                    r0 = 64 * kk + 32 * x
                    yb[slot, x, 0] = real[r0 : r0 + 32]
                    yb[slot, x, 1] = imag[r0 : r0 + 32]

    def send_first(jj, t):
        first = (z // 4 + t) % 2

        def send(i, carry):
            k, dest = first + 2 * (i // 4), (y + i) % 4
            dev = ((jnp.where(core == 0, xlo, 1 - xlo)) * 16 + z) * 4 + dest
            target = 2 * core + jj
            there = jnp.logical_or(dev != pa, target != sa)
            slot = (jj * 4 + k) * 4 + dest

            @pl.when(there)
            def _():
                pltpu.make_async_remote_copy(
                    yb.at[slot], xr.at[k, :, :, y], sx, rx.at[k],
                    device_id=(dev, target), device_id_type=MESH,
                ).start()

            @pl.when(jnp.logical_not(there))
            def _():
                pltpu.make_async_copy(yb.at[slot], xr.at[k, :, :, y], rx.at[k]).start()

            return carry

        lax.fori_loop(0, 8, send, 0)

    @pl.when(is_source)
    def _():
        correlate(w0, 0, 0)

    @pl.when(sa == 0)
    def _():
        pl.semaphore_wait(barrier, 38)

    @pl.when(sa == 1)
    def _():
        pl.semaphore_wait(barrier, 43)

    @pl.when(sa == 2)
    def _():
        pl.semaphore_wait(barrier, 35)

    @pl.when(sa == 3)
    def _():
        pl.semaphore_wait(barrier, 34)

    @pl.when(jnp.logical_or(sa == 1, sa == 2))
    def _():
        pltpu.make_async_remote_copy(
            halo_ref, hb, sh, rh,
            device_id=(pa, sa - 1), device_id_type=MESH,
        ).start()

    def row_send(i, carry):
        dev = here * 4 + (y + i) % 4
        pltpu.make_async_remote_copy(
            refs_ref, ga.at[y], srow, rrow, device_id=(dev, sa), device_id_type=MESH
        ).start()
        return carry

    lax.fori_loop(1, 4, row_send, 0)
    pltpu.make_async_copy(refs_ref, ga.at[y], rrow).start()

    eye = (
        lax.broadcasted_iota(jnp.int32, (128, 128), 0) == lax.broadcasted_iota(jnp.int32, (128, 128), 1)
    ).astype(BF16)

    def pass_on(k):
        pltpu.make_async_copy(xr.at[k], xr.at[k], rx.at[k]).wait()
        for x in range(2):
            pulses = xr[k, x].reshape(256, 128)
            flipped = lax.dot_general(eye, pulses, NT, preferred_element_type=F32).astype(BF16)
            for g in range(4):
                for c in range(2):
                    zs[16 * x + 4 * k + g, c] = flipped[32 * g : 32 * g + 32, 128 * c : 128 * c + 128]

        def send(i, carry):
            dest = (i // 4) * 16 + 4 * k + i % 4

            @pl.when(dest != here)
            def _():
                pltpu.make_async_remote_copy(
                    zs.at[dest], turned_ref.at[:, across * 16 + z], sz, rzs,
                    device_id=(dest * 4 + y, sa), device_id_type=MESH,
                ).start()

            @pl.when(dest == here)
            def _():
                pltpu.make_async_copy(zs.at[dest], turned_ref.at[:, across * 16 + z], rzs).start()

            return carry

        lax.fori_loop(0, 8, send, 0)

    @pl.when(is_source)
    def _():
        send_first(0, 0)
        correlate(w0, 0, 1)
        send_first(0, 1)
        for c in range(2):
            for r0 in (0, 16):
                tail = jnp.concatenate([planar_ref[c, r0 : r0 + 16, 4096:], jnp.zeros((16, HALO), BF16)], axis=1)
                w1[c, r0 : r0 + 16, :] = shifted(tail)
        pltpu.make_async_copy(hb, hb, rh).wait()
        w1[:, :, REACH - HALO :] = w1[:, :, REACH - HALO :] + hb[...]

        def second_half(t, carry):
            correlate(w1, 1, t)
            send_first(1, t)
            return carry

        lax.fori_loop(0, 2, second_half, 0)

    pltpu.make_async_copy(ga, ga, rrow).wait()
    wanted = jnp.dot(pick_ref[...], ga[...].reshape(64, 512), preferred_element_type=F32)
    for dest in range(32):
        rs[dest] = wanted[2 * dest : 2 * dest + 2]

    def row_pass(i, carry):
        dest = (here + i) % 32
        pltpu.make_async_remote_copy(
            rs.at[dest], rz.at[here], szrow, rzrow, device_id=(dest * 4 + y, sa), device_id_type=MESH
        ).start()
        return carry

    lax.fori_loop(1, 32, row_pass, 0)
    pltpu.make_async_copy(rs.at[here], rz.at[here], rzrow).start()

    def rest(t, carry):
        pass_on((z // 4 + t // 2) % 2 + 2 * (t % 2))
        return carry

    lax.fori_loop(0, 4, rest, 0)

    pltpu.make_async_copy(rz, rz, rzrow).wait()
    row_ref[...] = jnp.sum(rz[...], axis=0)

    pltpu.make_async_copy(turned_ref, turned_ref, rzs).wait()
    pltpu.make_async_copy(zs.at[pl.ds(0, 31)], zs.at[pl.ds(0, 31)], sz).wait()
    pltpu.make_async_copy(rs.at[pl.ds(0, 31)], rs.at[pl.ds(0, 31)], szrow).wait()
    pltpu.make_async_copy(ga.at[pl.ds(0, 3)], ga.at[pl.ds(0, 3)], srow).wait()

    @pl.when(jnp.logical_or(sa == 1, sa == 2))
    def _():
        pltpu.make_async_copy(halo_ref, halo_ref, sh).wait()

    @pl.when(sa == 0)
    def _():
        pltpu.make_async_copy(yb.at[pl.ds(0, 28)], yb.at[pl.ds(0, 28)], sx).wait()

    @pl.when(sa == 1)
    def _():
        pltpu.make_async_copy(yb, yb, sx).wait()


def azimuth_kernel(turned_ref, row_ref, out_ref, lhs, taps):
    zeros = jnp.zeros((32, 256), BF16)
    for c in range(2):
        lhs[c, 0] = zeros
        lhs[c, 17] = zeros
        for block in range(16):
            for half in range(2):
                tile = turned_ref[c, 2 * block + half]
                lhs[c, block + 1, :, 128 * half : 128 * half + 128] = tile
    for part in range(2):
        row = jnp.concatenate([row_ref[part : part + 1, :], jnp.zeros((1, 512), F32)], axis=1)
        wide = pltpu.roll(jnp.broadcast_to(row, (256, 1024)), 0, 1, stride=1, stride_axis=0)
        taps[256 * part : 256 * part + 256, :] = wide[:, :768].astype(BF16)
    got = []
    for c in range(2):
        total = None
        for o in range(3):
            rows = lhs[c, o : o + 16].reshape(512, 256)
            piece = lax.dot_general(rows, taps[:, 256 * o : 256 * o + 256], NT, preferred_element_type=F32)
            total = piece if total is None else total + piece
        got.append(total)
    real = got[0][:, :256] + got[1][:, 256:]
    imag = got[1][:, :256] - got[0][:, 256:]
    for block in range(16):
        out_ref[0, :, 256 * block : 256 * block + 256] = real[32 * block : 32 * block + 32]
        out_ref[1, :, 256 * block : 256 * block + 256] = imag[32 * block : 32 * block + 32]


def params(**more):
    return pltpu.CompilerParams(vmem_limit_bytes=20 << 20, **more)


def on_device(raw_echo, chirp_replica, azimuth_refs, migration_index, window_start):
    planar = jnp.transpose(raw_echo, (1, 0, 2))
    dma = pltpu.SemaphoreType.DMA
    turned, row = pl.pallas_call(
        turn_kernel,
        out_shape=(
            jax.ShapeDtypeStruct((2, 32, 32, 128), BF16),
            jax.ShapeDtypeStruct((2, 512), F32),
        ),
        in_specs=[SMEM, ANY, ANY, VMEM, ANY],
        out_specs=(ANY, VMEM),
        scratch_shapes=[
            pltpu.SMEM((4, 128), jnp.int32),
            pltpu.VMEM((2, 1024), BF16),
            pltpu.VMEM((4, 256, SPAN), BF16),
            pltpu.VMEM((64, 64), BF16),
            pltpu.VMEM((2, 32, REACH), BF16),
            pltpu.VMEM((2, 32, REACH), BF16),
            pltpu.VMEM((2, 32, HALO), BF16),
            pltpu.VMEM((2, 32, HALO), BF16),
            pltpu.VMEM((32, 2, 2, 32, 128), BF16),
            pltpu.VMEM((4, 2, 2, 4, 32, 128), BF16),
            pltpu.VMEM((32, 2, 32, 128), BF16),
            pltpu.VMEM((4, 8, 2, 512), BF16),
            pltpu.VMEM((32, 2, 512), F32),
            pltpu.VMEM((32, 2, 512), F32),
            dma((2,)), dma, dma, dma, dma((4,)), dma, dma, dma, dma, dma, dma,
        ],
        compiler_params=params(collective_id=0, has_side_effects=True),
        name="corner_turn",
    )(window_start, migration_index, chirp_replica, planar, azimuth_refs)

    image = pl.pallas_call(
        azimuth_kernel,
        out_shape=jax.ShapeDtypeStruct((2, 32, 4096), F32),
        in_specs=[VMEM, VMEM],
        out_specs=VMEM,
        scratch_shapes=[pltpu.VMEM((2, 18, 32, 256), BF16), pltpu.VMEM((512, 768), BF16)],
        compiler_params=params(),
        name="azimuth_correlate",
    )(turned, row)
    return jnp.transpose(image, (1, 0, 2))[None]


def solution(mesh):
    placed = (P("pa", None, "sa"), P(), P("pa", None, None), P(), P())
    return jax.shard_map(
        on_device, mesh=mesh, in_specs=placed, out_specs=P("sa", "pa", None, None), check_vma=False
    )
```

```python
import functools

import jax
import jax.numpy as jnp
from jax import lax
from jax.experimental import pallas as pl
from jax.experimental.pallas import tpu as pltpu
from jax.sharding import PartitionSpec as P

MESH = pl.DeviceIdType.MESH
BF16 = jnp.bfloat16
F32 = jnp.float32
NT = (((1,), (1,)), ((), ()))
SPAN = 1664
HALO = 3072
REACH = 5248
VMEM = pl.BlockSpec(memory_space=pltpu.VMEM)
SMEM = pl.BlockSpec(memory_space=pltpu.SMEM)
ANY = pl.BlockSpec(memory_space=pl.ANY)


def turn_kernel(
    start_ref, index_hbm, chirp_hbm, planar_ref, refs_ref, turned_ref, row_ref,
    index_ref, chirp_ref, taps_ref, pick_ref, w0, w1, halo_ref, hb, yb, xr, zs, ga, rs, rz, sin, sh, rh, sx, rx, sz, rzs, srow, rrow, szrow, rzrow,
):
    pa = lax.axis_index("pa")
    sa = lax.axis_index("sa")
    xlo, z, y = pa // 64, (pa // 4) % 16, pa % 4
    xhi, core = sa // 2, sa % 2
    here = xlo * 16 + z
    across = jnp.where(xhi == 0, xlo, 1 - xlo)
    is_source = xhi == 0

    get_index = pltpu.make_async_copy(index_hbm, index_ref, sin.at[0])
    get_chirp = pltpu.make_async_copy(chirp_hbm, chirp_ref, sin.at[1])
    get_index.start()
    get_chirp.start()

    barrier = pltpu.get_barrier_semaphore()

    def greet_source(i, carry):
        dev = (across * 16 + z) * 4 + i

        @pl.when(jnp.logical_or(dev != pa, xhi != sa))
        def _():
            pl.semaphore_signal(barrier, inc=1, device_id=(dev, xhi), device_id_type=MESH)

        return carry

    lax.fori_loop(0, 4, greet_source, 0)

    @pl.when(sa != 0)
    def _():
        def greet_y(i, carry):
            dev = here * 4 + (y + i) % 4
            pl.semaphore_signal(barrier, inc=1, device_id=(dev, sa), device_id_type=MESH)
            return carry

        lax.fori_loop(1, 4, greet_y, 0)

    def greet_line(i, carry):
        dev = ((here + i) % 32) * 4 + y
        pl.semaphore_signal(barrier, inc=1, device_id=(dev, sa), device_id_type=MESH)
        return carry

    lax.fori_loop(1, 32, greet_line, 0)

    @pl.when(sa < 2)
    def _():
        pl.semaphore_signal(barrier, inc=1, device_id=(pa, sa + 1), device_id_type=MESH)

    start = start_ref[0]
    bits = [jnp.bitwise_and(lax.shift_right_logical(start, bit), 1) == 1 for bit in range(11)]

    def shifted(value):
        for bit in (10, 9, 8, 7):
            step = 1 << bit
            value = jnp.where(bits[bit], value[:, step:], value[:, : value.shape[1] - step])
        return value

    get_chirp.wait()

    @pl.when(is_source)
    def _():
        for part in range(2):
            row = jnp.concatenate([chirp_ref[part : part + 1, :].astype(F32), jnp.zeros((1, 256), F32)], axis=1)
            row = jnp.broadcast_to(row, (8, 1280))
            for bit in range(7):
                row = jnp.where(bits[bit], pltpu.roll(row, 1 << bit, 1), row)
            wide = pltpu.roll(jnp.broadcast_to(row[:1], (128, 1280)), 0, 1, stride=1, stride_axis=0)
            wide = wide.astype(BF16)
            for dest in range(4):
                for g in range(4):
                    r0 = part * 128 + g * 32
                    if g > 0:
                        taps_ref[dest, r0 : r0 + 32, : 128 * g] = jnp.zeros((32, 128 * g), BF16)
                    taps_ref[dest, r0 : r0 + 32, 128 * g : 128 * g + 1280] = wide[32 * dest : 32 * dest + 32, :]
                    if g < 3:
                        taps_ref[dest, r0 : r0 + 32, 128 * g + 1280 :] = jnp.zeros((32, 384 - 128 * g), BF16)
        for c in range(2):
            for r0 in (0, 16):
                w0[c, r0 : r0 + 16, :] = shifted(planar_ref[c, r0 : r0 + 16, :7168])

    @pl.when(jnp.logical_or(sa == 1, sa == 2))
    def _():
        for c in range(2):
            for r0 in (0, 16):
                head = jnp.concatenate([jnp.zeros((16, 1920), BF16), planar_ref[c, r0 : r0 + 16, :HALO]], axis=1)
                halo_ref[c, r0 : r0 + 16, :] = shifted(head)

    get_index.wait()
    entry = lax.broadcasted_iota(jnp.int32, (64, 64), 0)
    code = jnp.full((64, 64), -2, jnp.int32)
    for dest in range(32):
        index = index_ref[sa, 4 * dest + y]
        code = jnp.where(entry // 2 == dest, jnp.where(index // 32 == pa // 4, 2 * (index % 32), -2), code)
    pick_ref[...] = (lax.broadcasted_iota(jnp.int32, (64, 64), 1) == code + entry % 2).astype(F32).astype(BF16)

    def correlate(window, jj, t):
        first = (z // 4 + t + 1) % 2
        pieces = []
        for c in range(2):
            for kk in range(2):
                for x in range(2):
                    off = pl.multiple_of(x * 2048 + (first + 2 * kk) * 512, 128)
                    pieces.append(window[c, :, pl.ds(off, SPAN)])
        lhs = jnp.concatenate(pieces, axis=0)
        for dest in range(4):
            got = lax.dot_general(lhs, taps_ref[dest], NT, preferred_element_type=F32)
            real = (got[:128, :128] + got[128:, 128:]).astype(BF16)
            imag = (got[128:, :128] - got[:128, 128:]).astype(BF16)
            for kk in range(2):
                slot = (jj * 4 + first + 2 * kk) * 4 + dest
                for x in range(2):
                    r0 = 64 * kk + 32 * x
                    yb[slot, x, 0] = real[r0 : r0 + 32]
                    yb[slot, x, 1] = imag[r0 : r0 + 32]

    def send_first(jj, t):
        first = (z // 4 + t + 1) % 2

        def send(i, carry):
            k, dest = first + 2 * (i // 4), (y + i) % 4
            dev = ((jnp.where(core == 0, xlo, 1 - xlo)) * 16 + z) * 4 + dest
            target = 2 * core + jj
            there = jnp.logical_or(dev != pa, target != sa)
            slot = (jj * 4 + k) * 4 + dest

            @pl.when(there)
            def _():
                pltpu.make_async_remote_copy(
                    yb.at[slot], xr.at[k, :, :, y], sx, rx.at[k],
                    device_id=(dev, target), device_id_type=MESH,
                ).start()

            @pl.when(jnp.logical_not(there))
            def _():
                pltpu.make_async_copy(yb.at[slot], xr.at[k, :, :, y], rx.at[k]).start()

            return carry

        lax.fori_loop(0, 8, send, 0)

    @pl.when(is_source)
    def _():
        def first_half(t, carry):
            correlate(w0, 0, t)
            return carry

        lax.fori_loop(0, 2, first_half, 0)
        for c in range(2):
            for r0 in (0, 16):
                tail = jnp.concatenate([planar_ref[c, r0 : r0 + 16, 4096:], jnp.zeros((16, HALO), BF16)], axis=1)
                w1[c, r0 : r0 + 16, :] = shifted(tail)

    @pl.when(sa == 0)
    def _():
        pl.semaphore_wait(barrier, 38)

    @pl.when(sa == 1)
    def _():
        pl.semaphore_wait(barrier, 43)

    @pl.when(sa == 2)
    def _():
        pl.semaphore_wait(barrier, 35)

    @pl.when(sa == 3)
    def _():
        pl.semaphore_wait(barrier, 34)

    @pl.when(jnp.logical_or(sa == 1, sa == 2))
    def _():
        pltpu.make_async_remote_copy(
            halo_ref, hb, sh, rh,
            device_id=(pa, sa - 1), device_id_type=MESH,
        ).start()

    def row_send(i, carry):
        dev = here * 4 + (y + i) % 4
        pltpu.make_async_remote_copy(
            refs_ref, ga.at[y], srow, rrow, device_id=(dev, sa), device_id_type=MESH
        ).start()
        return carry

    lax.fori_loop(1, 4, row_send, 0)
    pltpu.make_async_copy(refs_ref, ga.at[y], rrow).start()

    eye = (
        lax.broadcasted_iota(jnp.int32, (128, 128), 0) == lax.broadcasted_iota(jnp.int32, (128, 128), 1)
    ).astype(BF16)

    def far_first(t):
        return (z // 4 + jnp.where(t < 2, 1 + 2 * t, 6 - 2 * t)) % 4

    def pass_on(k):
        pltpu.make_async_copy(xr.at[k], xr.at[k], rx.at[k]).wait()
        for x in range(2):
            pulses = xr[k, x].reshape(256, 128)
            flipped = lax.dot_general(eye, pulses, NT, preferred_element_type=F32).astype(BF16)
            for g in range(4):
                for c in range(2):
                    zs[16 * x + 4 * k + g, c] = flipped[32 * g : 32 * g + 32, 128 * c : 128 * c + 128]

        def send(i, carry):
            dest = (i // 4) * 16 + 4 * k + i % 4

            @pl.when(dest != here)
            def _():
                pltpu.make_async_remote_copy(
                    zs.at[dest], turned_ref.at[:, across * 16 + z], sz, rzs,
                    device_id=(dest * 4 + y, sa), device_id_type=MESH,
                ).start()

            @pl.when(dest == here)
            def _():
                pltpu.make_async_copy(zs.at[dest], turned_ref.at[:, across * 16 + z], rzs).start()

            return carry

        lax.fori_loop(0, 8, send, 0)

    @pl.when(is_source)
    def _():
        send_first(0, 0)
        send_first(0, 1)

        def second_half(t, carry):
            @pl.when(sa == 0)
            def _():
                pass_on(far_first(2 * t))
                pass_on(far_first(2 * t + 1))

            @pl.when(t == 0)
            def _():
                pltpu.make_async_copy(hb, hb, rh).wait()
                w1[:, :, REACH - HALO :] = w1[:, :, REACH - HALO :] + hb[...]

            correlate(w1, 1, t)
            send_first(1, t)
            return carry

        lax.fori_loop(0, 2, second_half, 0)

    pltpu.make_async_copy(ga, ga, rrow).wait()
    wanted = jnp.dot(pick_ref[...], ga[...].reshape(64, 512), preferred_element_type=F32)
    for dest in range(32):
        rs[dest] = wanted[2 * dest : 2 * dest + 2]

    def row_pass(i, carry):
        dest = (here + i) % 32
        pltpu.make_async_remote_copy(
            rs.at[dest], rz.at[here], szrow, rzrow, device_id=(dest * 4 + y, sa), device_id_type=MESH
        ).start()
        return carry

    lax.fori_loop(1, 32, row_pass, 0)
    pltpu.make_async_copy(rs.at[here], rz.at[here], rzrow).start()

    def rest(t, carry):
        pass_on(far_first(t))
        return carry

    lax.fori_loop(jnp.where(sa == 0, 4, 0), 4, rest, 0)

    pltpu.make_async_copy(rz, rz, rzrow).wait()
    row_ref[...] = jnp.sum(rz[...], axis=0)

    pltpu.make_async_copy(turned_ref, turned_ref, rzs).wait()
    pltpu.make_async_copy(zs.at[pl.ds(0, 31)], zs.at[pl.ds(0, 31)], sz).wait()
    pltpu.make_async_copy(rs.at[pl.ds(0, 31)], rs.at[pl.ds(0, 31)], szrow).wait()
    pltpu.make_async_copy(ga.at[pl.ds(0, 3)], ga.at[pl.ds(0, 3)], srow).wait()

    @pl.when(jnp.logical_or(sa == 1, sa == 2))
    def _():
        pltpu.make_async_copy(halo_ref, halo_ref, sh).wait()

    @pl.when(sa == 0)
    def _():
        pltpu.make_async_copy(yb.at[pl.ds(0, 28)], yb.at[pl.ds(0, 28)], sx).wait()

    @pl.when(sa == 1)
    def _():
        pltpu.make_async_copy(yb, yb, sx).wait()


def azimuth_kernel(turned_ref, row_ref, out_ref, lhs, taps):
    zeros = jnp.zeros((32, 256), BF16)
    for c in range(2):
        lhs[c, 0] = zeros
        lhs[c, 17] = zeros
        for block in range(16):
            for half in range(2):
                tile = turned_ref[c, 2 * block + half]
                lhs[c, block + 1, :, 128 * half : 128 * half + 128] = tile
    for part in range(2):
        row = jnp.concatenate([row_ref[part : part + 1, :], jnp.zeros((1, 512), F32)], axis=1)
        wide = pltpu.roll(jnp.broadcast_to(row, (256, 1024)), 0, 1, stride=1, stride_axis=0)
        taps[256 * part : 256 * part + 256, :] = wide[:, :768].astype(BF16)
    got = []
    for c in range(2):
        total = None
        for o in range(3):
            rows = lhs[c, o : o + 16].reshape(512, 256)
            piece = lax.dot_general(rows, taps[:, 256 * o : 256 * o + 256], NT, preferred_element_type=F32)
            total = piece if total is None else total + piece
        got.append(total)
    real = got[0][:, :256] + got[1][:, 256:]
    imag = got[1][:, :256] - got[0][:, 256:]
    for block in range(16):
        out_ref[0, :, 256 * block : 256 * block + 256] = real[32 * block : 32 * block + 32]
        out_ref[1, :, 256 * block : 256 * block + 256] = imag[32 * block : 32 * block + 32]


def params(**more):
    return pltpu.CompilerParams(vmem_limit_bytes=20 << 20, **more)


def on_device(raw_echo, chirp_replica, azimuth_refs, migration_index, window_start):
    planar = jnp.transpose(raw_echo, (1, 0, 2))
    dma = pltpu.SemaphoreType.DMA
    turned, row = pl.pallas_call(
        turn_kernel,
        out_shape=(
            jax.ShapeDtypeStruct((2, 32, 32, 128), BF16),
            jax.ShapeDtypeStruct((2, 512), F32),
        ),
        in_specs=[SMEM, ANY, ANY, VMEM, ANY],
        out_specs=(ANY, VMEM),
        scratch_shapes=[
            pltpu.SMEM((4, 128), jnp.int32),
            pltpu.VMEM((2, 1024), BF16),
            pltpu.VMEM((4, 256, SPAN), BF16),
            pltpu.VMEM((64, 64), BF16),
            pltpu.VMEM((2, 32, REACH), BF16),
            pltpu.VMEM((2, 32, REACH), BF16),
            pltpu.VMEM((2, 32, HALO), BF16),
            pltpu.VMEM((2, 32, HALO), BF16),
            pltpu.VMEM((32, 2, 2, 32, 128), BF16),
            pltpu.VMEM((4, 2, 2, 4, 32, 128), BF16),
            pltpu.VMEM((32, 2, 32, 128), BF16),
            pltpu.VMEM((4, 8, 2, 512), BF16),
            pltpu.VMEM((32, 2, 512), F32),
            pltpu.VMEM((32, 2, 512), F32),
            dma((2,)), dma, dma, dma, dma((4,)), dma, dma, dma, dma, dma, dma,
        ],
        compiler_params=params(collective_id=0, has_side_effects=True),
        name="corner_turn",
    )(window_start, migration_index, chirp_replica, planar, azimuth_refs)

    image = pl.pallas_call(
        azimuth_kernel,
        out_shape=jax.ShapeDtypeStruct((2, 32, 4096), F32),
        in_specs=[VMEM, VMEM],
        out_specs=VMEM,
        scratch_shapes=[pltpu.VMEM((2, 18, 32, 256), BF16), pltpu.VMEM((512, 768), BF16)],
        compiler_params=params(),
        name="azimuth_correlate",
    )(turned, row)
    return jnp.transpose(image, (1, 0, 2))[None]


def solution(mesh):
    placed = (P("pa", None, "sa"), P(), P("pa", None, None), P(), P())
    return jax.shard_map(
        on_device, mesh=mesh, in_specs=placed, out_specs=P("sa", "pa", None, None), check_vma=False
    )
```

```python
import functools

import jax
import jax.numpy as jnp
from jax import lax
from jax.experimental import pallas as pl
from jax.experimental.pallas import tpu as pltpu
from jax.sharding import PartitionSpec as P

MESH = pl.DeviceIdType.MESH
BF16 = jnp.bfloat16
F32 = jnp.float32
NT = (((1,), (1,)), ((), ()))
SPAN = 1664
HALO = 3072
REACH = 5248
VMEM = pl.BlockSpec(memory_space=pltpu.VMEM)
SMEM = pl.BlockSpec(memory_space=pltpu.SMEM)
ANY = pl.BlockSpec(memory_space=pl.ANY)


def turn_kernel(
    start_ref, index_hbm, chirp_hbm, planar_ref, refs_ref, turned_ref, row_ref,
    index_ref, chirp_ref, taps_ref, pick_ref, w0, w1, halo_ref, hb, yb, xr, zs, ga, rs, rz, sin, sh, rh, sx, rx, sz, rzs, srow, rrow, szrow, rzrow,
):
    pa = lax.axis_index("pa")
    sa = lax.axis_index("sa")
    xlo, z, y = pa // 64, (pa // 4) % 16, pa % 4
    xhi, core = sa // 2, sa % 2
    here = xlo * 16 + z
    across = jnp.where(xhi == 0, xlo, 1 - xlo)
    is_source = xhi == 0
    place = xlo * 4 + y

    get_index = pltpu.make_async_copy(index_hbm, index_ref, sin.at[0])
    get_chirp = pltpu.make_async_copy(chirp_hbm, chirp_ref, sin.at[1])
    get_index.start()
    get_chirp.start()

    barrier = pltpu.get_barrier_semaphore()

    @pl.when(sa != 0)
    def _():
        def greet_source(i, carry):
            dev = (across * 16 + z) * 4 + i
            pl.semaphore_signal(barrier, inc=1, device_id=(dev, xhi), device_id_type=MESH)
            return carry

        lax.fori_loop(0, 4, greet_source, 0)

    def greet_plane(i, carry):
        dev = ((i // 3) * 16 + z) * 4 + (y + 1 + i % 3) % 4
        pl.semaphore_signal(barrier, inc=1, device_id=(dev, sa), device_id_type=MESH)
        return carry

    lax.fori_loop(0, 6, greet_plane, 0)

    def greet_line(i, carry):
        dev = ((here + i) % 32) * 4 + y
        pl.semaphore_signal(barrier, inc=1, device_id=(dev, sa), device_id_type=MESH)
        return carry

    lax.fori_loop(1, 32, greet_line, 0)

    @pl.when(sa < 2)
    def _():
        pl.semaphore_signal(barrier, inc=1, device_id=(pa, sa + 1), device_id_type=MESH)

    start = start_ref[0]
    bits = [jnp.bitwise_and(lax.shift_right_logical(start, bit), 1) == 1 for bit in range(11)]

    def shifted(value):
        for bit in (10, 9, 8, 7):
            step = 1 << bit
            value = jnp.where(bits[bit], value[:, step:], value[:, : value.shape[1] - step])
        return value

    get_chirp.wait()

    @pl.when(is_source)
    def _():
        for part in range(2):
            row = jnp.concatenate([chirp_ref[part : part + 1, :].astype(F32), jnp.zeros((1, 256), F32)], axis=1)
            row = jnp.broadcast_to(row, (8, 1280))
            for bit in range(7):
                row = jnp.where(bits[bit], pltpu.roll(row, 1 << bit, 1), row)
            wide = pltpu.roll(jnp.broadcast_to(row[:1], (128, 1280)), 0, 1, stride=1, stride_axis=0)
            wide = wide.astype(BF16)
            for dest in range(4):
                for g in range(4):
                    r0 = part * 128 + g * 32
                    if g > 0:
                        taps_ref[dest, r0 : r0 + 32, : 128 * g] = jnp.zeros((32, 128 * g), BF16)
                    taps_ref[dest, r0 : r0 + 32, 128 * g : 128 * g + 1280] = wide[32 * dest : 32 * dest + 32, :]
                    if g < 3:
                        taps_ref[dest, r0 : r0 + 32, 128 * g + 1280 :] = jnp.zeros((32, 384 - 128 * g), BF16)
        for c in range(2):
            for r0 in (0, 16):
                w0[c, r0 : r0 + 16, :] = shifted(planar_ref[c, r0 : r0 + 16, :7168])

    @pl.when(jnp.logical_or(sa == 1, sa == 2))
    def _():
        for c in range(2):
            for r0 in (0, 16):
                head = jnp.concatenate([jnp.zeros((16, 1920), BF16), planar_ref[c, r0 : r0 + 16, :HALO]], axis=1)
                halo_ref[c, r0 : r0 + 16, :] = shifted(head)

    get_index.wait()
    entry = lax.broadcasted_iota(jnp.int32, (32, 128), 0)
    code = jnp.full((32, 128), -2, jnp.int32)
    for dest in range(16):
        index = index_ref[sa, xlo * 64 + 4 * dest + y]
        slot = (index // 512) * 32 + index % 32
        code = jnp.where(entry // 2 == dest, jnp.where((index // 32) % 16 == z, 2 * slot, -2), code)
    pick_ref[...] = (lax.broadcasted_iota(jnp.int32, (32, 128), 1) == code + entry % 2).astype(F32).astype(BF16)

    def correlate(window, jj, t):
        first = (z // 4 + t + 1) % 2
        pieces = []
        for c in range(2):
            for kk in range(2):
                for x in range(2):
                    off = pl.multiple_of(x * 2048 + (first + 2 * kk) * 512, 128)
                    pieces.append(window[c, :, pl.ds(off, SPAN)])
        lhs = jnp.concatenate(pieces, axis=0)
        for dest in range(4):
            got = lax.dot_general(lhs, taps_ref[dest], NT, preferred_element_type=F32)
            real = (got[:128, :128] + got[128:, 128:]).astype(BF16)
            imag = (got[128:, :128] - got[:128, 128:]).astype(BF16)
            for kk in range(2):
                slot = (jj * 4 + first + 2 * kk) * 4 + dest
                for x in range(2):
                    r0 = 64 * kk + 32 * x
                    yb[slot, x, 0] = real[r0 : r0 + 32]
                    yb[slot, x, 1] = imag[r0 : r0 + 32]

    def send_first(jj, t):
        first = (z // 4 + t + 1) % 2

        def send(i, carry):
            k, dest = first + 2 * (i // 4), (y + i) % 4
            dev = ((jnp.where(core == 0, xlo, 1 - xlo)) * 16 + z) * 4 + dest
            target = 2 * core + jj
            there = jnp.logical_or(dev != pa, target != sa)
            slot = (jj * 4 + k) * 4 + dest

            @pl.when(there)
            def _():
                pltpu.make_async_remote_copy(
                    yb.at[slot], xr.at[k, :, :, y], sx, rx.at[k],
                    device_id=(dev, target), device_id_type=MESH,
                ).start()

            @pl.when(jnp.logical_not(there))
            def _():
                pltpu.make_async_copy(yb.at[slot], xr.at[k, :, :, y], rx.at[k]).start()

            return carry

        lax.fori_loop(0, 8, send, 0)

    @pl.when(is_source)
    def _():
        def first_half(t, carry):
            correlate(w0, 0, t)
            return carry

        lax.fori_loop(0, 2, first_half, 0)
        for c in range(2):
            for r0 in (0, 16):
                tail = jnp.concatenate([planar_ref[c, r0 : r0 + 16, 4096:], jnp.zeros((16, HALO), BF16)], axis=1)
                w1[c, r0 : r0 + 16, :] = shifted(tail)

    @pl.when(sa == 0)
    def _():
        pl.semaphore_wait(barrier, 41)

    @pl.when(sa == 1)
    def _():
        pl.semaphore_wait(barrier, 46)

    @pl.when(sa == 2)
    def _():
        pl.semaphore_wait(barrier, 38)

    @pl.when(sa == 3)
    def _():
        pl.semaphore_wait(barrier, 37)

    @pl.when(jnp.logical_or(sa == 1, sa == 2))
    def _():
        pltpu.make_async_remote_copy(
            halo_ref, hb, sh, rh,
            device_id=(pa, sa - 1), device_id_type=MESH,
        ).start()

    def row_send(i, carry):
        there = (place + i) % 8
        pltpu.make_async_remote_copy(
            refs_ref, ga.at[place], srow, rrow,
            device_id=(((there // 4) * 16 + z) * 4 + there % 4, sa), device_id_type=MESH,
        ).start()
        return carry

    lax.fori_loop(1, 8, row_send, 0)
    pltpu.make_async_copy(refs_ref, ga.at[place], rrow).start()

    eye = (
        lax.broadcasted_iota(jnp.int32, (128, 128), 0) == lax.broadcasted_iota(jnp.int32, (128, 128), 1)
    ).astype(BF16)

    def far_first(t):
        return (z // 4 + jnp.where(t < 2, 1 + 2 * t, 6 - 2 * t)) % 4

    def pass_on(k):
        pltpu.make_async_copy(xr.at[k], xr.at[k], rx.at[k]).wait()
        for x in range(2):
            pulses = xr[k, x].reshape(256, 128)
            flipped = lax.dot_general(eye, pulses, NT, preferred_element_type=F32).astype(BF16)
            for g in range(4):
                for c in range(2):
                    zs[16 * x + 4 * k + g, c] = flipped[32 * g : 32 * g + 32, 128 * c : 128 * c + 128]

        def send(i, carry):
            dest = (i // 4) * 16 + 4 * k + i % 4

            @pl.when(dest != here)
            def _():
                pltpu.make_async_remote_copy(
                    zs.at[dest], turned_ref.at[:, across * 16 + z], sz, rzs,
                    device_id=(dest * 4 + y, sa), device_id_type=MESH,
                ).start()

            @pl.when(dest == here)
            def _():
                pltpu.make_async_copy(zs.at[dest], turned_ref.at[:, across * 16 + z], rzs).start()

            return carry

        lax.fori_loop(0, 8, send, 0)

    @pl.when(is_source)
    def _():
        send_first(0, 0)
        send_first(0, 1)

        def second_half(t, carry):
            @pl.when(sa == 0)
            def _():
                pass_on(far_first(2 * t))
                pass_on(far_first(2 * t + 1))

            @pl.when(t == 0)
            def _():
                pltpu.make_async_copy(hb, hb, rh).wait()
                w1[:, :, REACH - HALO :] = w1[:, :, REACH - HALO :] + hb[...]

            correlate(w1, 1, t)
            send_first(1, t)
            return carry

        lax.fori_loop(0, 2, second_half, 0)

    pltpu.make_async_copy(ga, ga, rrow).wait()
    wanted = jnp.dot(pick_ref[...], ga[...].reshape(128, 512), preferred_element_type=F32)
    for dest in range(16):
        rs[dest] = wanted[2 * dest : 2 * dest + 2].astype(BF16)

    def row_pass(i, carry):
        dest = (z + i) % 16
        pltpu.make_async_remote_copy(
            rs.at[dest], rz.at[z], szrow, rzrow,
            device_id=((xlo * 16 + dest) * 4 + y, sa), device_id_type=MESH,
        ).start()
        return carry

    lax.fori_loop(1, 16, row_pass, 0)
    pltpu.make_async_copy(rs.at[z], rz.at[z], rzrow).start()

    def rest(t, carry):
        pass_on(far_first(t))
        return carry

    lax.fori_loop(jnp.where(sa == 0, 4, 0), 4, rest, 0)

    pltpu.make_async_copy(rz, rz, rzrow).wait()
    row_ref[...] = jnp.sum(rz[...].astype(F32), axis=0)

    pltpu.make_async_copy(turned_ref, turned_ref, rzs).wait()
    pltpu.make_async_copy(zs.at[pl.ds(0, 31)], zs.at[pl.ds(0, 31)], sz).wait()
    pltpu.make_async_copy(rs.at[pl.ds(0, 15)], rs.at[pl.ds(0, 15)], szrow).wait()
    pltpu.make_async_copy(ga.at[pl.ds(0, 7)], ga.at[pl.ds(0, 7)], srow).wait()

    @pl.when(jnp.logical_or(sa == 1, sa == 2))
    def _():
        pltpu.make_async_copy(halo_ref, halo_ref, sh).wait()

    @pl.when(sa == 0)
    def _():
        pltpu.make_async_copy(yb.at[pl.ds(0, 28)], yb.at[pl.ds(0, 28)], sx).wait()

    @pl.when(sa == 1)
    def _():
        pltpu.make_async_copy(yb, yb, sx).wait()


def azimuth_kernel(turned_ref, row_ref, out_ref, lhs, taps):
    zeros = jnp.zeros((32, 256), BF16)
    for c in range(2):
        lhs[c, 0] = zeros
        lhs[c, 17] = zeros
        for block in range(16):
            for half in range(2):
                tile = turned_ref[c, 2 * block + half]
                lhs[c, block + 1, :, 128 * half : 128 * half + 128] = tile
    for part in range(2):
        row = jnp.concatenate([row_ref[part : part + 1, :], jnp.zeros((1, 512), F32)], axis=1)
        wide = pltpu.roll(jnp.broadcast_to(row, (256, 1024)), 0, 1, stride=1, stride_axis=0)
        taps[256 * part : 256 * part + 256, :] = wide[:, :768].astype(BF16)
    got = []
    for c in range(2):
        total = None
        for o in range(3):
            rows = lhs[c, o : o + 16].reshape(512, 256)
            piece = lax.dot_general(rows, taps[:, 256 * o : 256 * o + 256], NT, preferred_element_type=F32)
            total = piece if total is None else total + piece
        got.append(total)
    real = got[0][:, :256] + got[1][:, 256:]
    imag = got[1][:, :256] - got[0][:, 256:]
    for block in range(16):
        out_ref[:, 0, 256 * block : 256 * block + 256] = real[32 * block : 32 * block + 32]
        out_ref[:, 1, 256 * block : 256 * block + 256] = imag[32 * block : 32 * block + 32]


def params(**more):
    return pltpu.CompilerParams(vmem_limit_bytes=20 << 20, **more)


def on_device(raw_echo, chirp_replica, azimuth_refs, migration_index, window_start):
    planar = jnp.transpose(raw_echo, (1, 0, 2))
    dma = pltpu.SemaphoreType.DMA
    turned, row = pl.pallas_call(
        turn_kernel,
        out_shape=(
            jax.ShapeDtypeStruct((2, 32, 32, 128), BF16),
            jax.ShapeDtypeStruct((2, 512), F32),
        ),
        in_specs=[SMEM, ANY, ANY, VMEM, ANY],
        out_specs=(ANY, VMEM),
        scratch_shapes=[
            pltpu.SMEM((4, 128), jnp.int32),
            pltpu.VMEM((2, 1024), BF16),
            pltpu.VMEM((4, 256, SPAN), BF16),
            pltpu.VMEM((32, 128), BF16),
            pltpu.VMEM((2, 32, REACH), BF16),
            pltpu.VMEM((2, 32, REACH), BF16),
            pltpu.VMEM((2, 32, HALO), BF16),
            pltpu.VMEM((2, 32, HALO), BF16),
            pltpu.VMEM((32, 2, 2, 32, 128), BF16),
            pltpu.VMEM((4, 2, 2, 4, 32, 128), BF16),
            pltpu.VMEM((32, 2, 32, 128), BF16),
            pltpu.VMEM((8, 8, 2, 512), BF16),
            pltpu.VMEM((16, 2, 512), BF16),
            pltpu.VMEM((16, 2, 512), BF16),
            dma((2,)), dma, dma, dma, dma((4,)), dma, dma, dma, dma, dma, dma,
        ],
        compiler_params=params(collective_id=0, has_side_effects=True),
        name="corner_turn",
    )(window_start, migration_index, chirp_replica, planar, azimuth_refs)

    image = pl.pallas_call(
        azimuth_kernel,
        out_shape=jax.ShapeDtypeStruct((32, 2, 4096), F32),
        in_specs=[VMEM, VMEM],
        out_specs=VMEM,
        scratch_shapes=[pltpu.VMEM((2, 18, 32, 256), BF16), pltpu.VMEM((512, 768), BF16)],
        compiler_params=params(),
        name="azimuth_correlate",
    )(turned, row)
    return image[None]


def solution(mesh):
    placed = (P("pa", None, "sa"), P(), P("pa", None, None), P(), P())
    return jax.shard_map(
        on_device, mesh=mesh, in_specs=placed, out_specs=P("sa", "pa", None, None), check_vma=False
    )
```

```python
import functools

import jax
import jax.numpy as jnp
from jax import lax
from jax.experimental import pallas as pl
from jax.experimental.pallas import tpu as pltpu
from jax.sharding import PartitionSpec as P

MESH = pl.DeviceIdType.MESH
BF16 = jnp.bfloat16
F32 = jnp.float32
NT = (((1,), (1,)), ((), ()))
SPAN = 1664
HALO = 3072
REACH = 5248
VMEM = pl.BlockSpec(memory_space=pltpu.VMEM)
SMEM = pl.BlockSpec(memory_space=pltpu.SMEM)
ANY = pl.BlockSpec(memory_space=pl.ANY)
HBM = pl.BlockSpec(memory_space=pltpu.HBM)


def turn_kernel(
    start_ref, index_hbm, chirp_hbm, raw_hbm, refs_ref, turned_ref, row_ref,
    raw_ref, planar_ref, index_ref, chirp_ref, taps_ref, pick_ref, w0, w1, halo_ref, hb, yb, xr, zs, ga, rs, rz, sraw, sin, sh, rh, sx, rx, sz, rzs, srow, rrow, szrow, rzrow,
):
    pa = lax.axis_index("pa")
    sa = lax.axis_index("sa")
    xlo, z, y = pa // 64, (pa // 4) % 16, pa % 4
    xhi, core = sa // 2, sa % 2
    here = xlo * 16 + z
    across = jnp.where(xhi == 0, xlo, 1 - xlo)
    is_source = xhi == 0
    place = xlo * 4 + y

    get_index = pltpu.make_async_copy(index_hbm, index_ref, sin.at[0])
    get_chirp = pltpu.make_async_copy(chirp_hbm, chirp_ref, sin.at[1])
    get_chirp.start()
    get_index.start()

    def get_raw(q):
        part = pl.ds(2048 * q, 2048)
        return pltpu.make_async_copy(raw_hbm.at[:, :, part], raw_ref.at[:, :, part], sraw.at[q])

    for q in range(4):
        get_raw(q).start()

    barrier = pltpu.get_barrier_semaphore()

    @pl.when(sa != 0)
    def _():
        def greet_source(i, carry):
            dev = (across * 16 + z) * 4 + i
            pl.semaphore_signal(barrier, inc=1, device_id=(dev, xhi), device_id_type=MESH)
            return carry

        lax.fori_loop(0, 4, greet_source, 0)

    def greet_plane(i, carry):
        dev = ((i // 3) * 16 + z) * 4 + (y + 1 + i % 3) % 4
        pl.semaphore_signal(barrier, inc=1, device_id=(dev, sa), device_id_type=MESH)
        return carry

    lax.fori_loop(0, 6, greet_plane, 0)

    def greet_line(i, carry):
        dev = ((here + i) % 32) * 4 + y
        pl.semaphore_signal(barrier, inc=1, device_id=(dev, sa), device_id_type=MESH)
        return carry

    lax.fori_loop(1, 32, greet_line, 0)

    @pl.when(sa < 2)
    def _():
        pl.semaphore_signal(barrier, inc=1, device_id=(pa, sa + 1), device_id_type=MESH)

    start = start_ref[0]
    bits = [jnp.bitwise_and(lax.shift_right_logical(start, bit), 1) == 1 for bit in range(11)]

    def shifted(value):
        for bit in (10, 9, 8, 7):
            step = 1 << bit
            value = jnp.where(bits[bit], value[:, step:], value[:, : value.shape[1] - step])
        return value

    get_chirp.wait()

    @pl.when(is_source)
    def _():
        for part in range(2):
            row = jnp.concatenate([chirp_ref[part : part + 1, :].astype(F32), jnp.zeros((1, 256), F32)], axis=1)
            row = jnp.broadcast_to(row, (8, 1280))
            for bit in range(7):
                row = jnp.where(bits[bit], pltpu.roll(row, 1 << bit, 1), row)
            wide = pltpu.roll(jnp.broadcast_to(row[:1], (128, 1280)), 0, 1, stride=1, stride_axis=0)
            wide = wide.astype(BF16)
            for dest in range(4):
                for g in range(4):
                    r0 = part * 128 + g * 32
                    if g > 0:
                        taps_ref[dest, r0 : r0 + 32, : 128 * g] = jnp.zeros((32, 128 * g), BF16)
                    taps_ref[dest, r0 : r0 + 32, 128 * g : 128 * g + 1280] = wide[32 * dest : 32 * dest + 32, :]
                    if g < 3:
                        taps_ref[dest, r0 : r0 + 32, 128 * g + 1280 :] = jnp.zeros((32, 384 - 128 * g), BF16)

    get_index.wait()
    entry = lax.broadcasted_iota(jnp.int32, (32, 128), 0)
    code = jnp.full((32, 128), -2, jnp.int32)
    for dest in range(16):
        index = index_ref[sa, xlo * 64 + 4 * dest + y]
        slot = (index // 512) * 32 + index % 32
        code = jnp.where(entry // 2 == dest, jnp.where((index // 32) % 16 == z, 2 * slot, -2), code)
    pick_ref[...] = (lax.broadcasted_iota(jnp.int32, (32, 128), 1) == code + entry % 2).astype(F32).astype(BF16)

    source_row = lax.broadcasted_iota(jnp.int32, (64, 64), 1)
    target_row = lax.broadcasted_iota(jnp.int32, (64, 64), 0)
    apart = (source_row == 2 * (target_row % 32) + target_row // 32).astype(F32).astype(BF16)
    for q in range(4):
        get_raw(q).wait()
        rows = raw_ref[:, :, 2048 * q : 2048 * q + 2048].reshape(64, 2048)
        rows = jnp.dot(apart, rows, preferred_element_type=F32).astype(BF16)
        planar_ref[0, :, 2048 * q : 2048 * q + 2048] = rows[:32]
        planar_ref[1, :, 2048 * q : 2048 * q + 2048] = rows[32:]

    @pl.when(jnp.logical_or(sa == 1, sa == 2))
    def _():
        for c in range(2):
            for r0 in (0, 16):
                head = jnp.concatenate([jnp.zeros((16, 1920), BF16), planar_ref[c, r0 : r0 + 16, :HALO]], axis=1)
                halo_ref[c, r0 : r0 + 16, :] = shifted(head)

    def correlate(window, jj, t):
        first = (z // 4 + t + 1) % 2
        pieces = []
        for c in range(2):
            for kk in range(2):
                for x in range(2):
                    off = pl.multiple_of(x * 2048 + (first + 2 * kk) * 512, 128)
                    pieces.append(window[c, :, pl.ds(off, SPAN)])
        lhs = jnp.concatenate(pieces, axis=0)
        for dest in range(4):
            got = lax.dot_general(lhs, taps_ref[dest], NT, preferred_element_type=F32)
            real = (got[:128, :128] + got[128:, 128:]).astype(BF16)
            imag = (got[128:, :128] - got[:128, 128:]).astype(BF16)
            for kk in range(2):
                slot = (jj * 4 + first + 2 * kk) * 4 + dest
                for x in range(2):
                    r0 = 64 * kk + 32 * x
                    yb[slot, x, 0] = real[r0 : r0 + 32]
                    yb[slot, x, 1] = imag[r0 : r0 + 32]

    def send_first(jj, t):
        first = (z // 4 + t + 1) % 2

        def send(i, carry):
            k, dest = first + 2 * (i // 4), (y + i) % 4
            dev = ((jnp.where(core == 0, xlo, 1 - xlo)) * 16 + z) * 4 + dest
            target = 2 * core + jj
            there = jnp.logical_or(dev != pa, target != sa)
            slot = (jj * 4 + k) * 4 + dest

            @pl.when(there)
            def _():
                pltpu.make_async_remote_copy(
                    yb.at[slot], xr.at[k, :, :, y], sx, rx.at[k],
                    device_id=(dev, target), device_id_type=MESH,
                ).start()

            @pl.when(jnp.logical_not(there))
            def _():
                pltpu.make_async_copy(yb.at[slot], xr.at[k, :, :, y], rx.at[k]).start()

            return carry

        lax.fori_loop(0, 8, send, 0)

    @pl.when(is_source)
    def _():
        for c in range(2):
            for r0 in (0, 16):
                w0[c, r0 : r0 + 16, :] = shifted(planar_ref[c, r0 : r0 + 16, :7168])

        def first_half(t, carry):
            correlate(w0, 0, t)
            return carry

        lax.fori_loop(0, 2, first_half, 0)
        for c in range(2):
            for r0 in (0, 16):
                tail = jnp.concatenate([planar_ref[c, r0 : r0 + 16, 4096:], jnp.zeros((16, HALO), BF16)], axis=1)
                w1[c, r0 : r0 + 16, :] = shifted(tail)

    @pl.when(sa == 0)
    def _():
        pl.semaphore_wait(barrier, 41)

    @pl.when(sa == 1)
    def _():
        pl.semaphore_wait(barrier, 46)

    @pl.when(sa == 2)
    def _():
        pl.semaphore_wait(barrier, 38)

    @pl.when(sa == 3)
    def _():
        pl.semaphore_wait(barrier, 37)

    @pl.when(jnp.logical_or(sa == 1, sa == 2))
    def _():
        pltpu.make_async_remote_copy(
            halo_ref, hb, sh, rh,
            device_id=(pa, sa - 1), device_id_type=MESH,
        ).start()

    def row_send(i, carry):
        there = (place + i) % 8
        pltpu.make_async_remote_copy(
            refs_ref, ga.at[place], srow, rrow,
            device_id=(((there // 4) * 16 + z) * 4 + there % 4, sa), device_id_type=MESH,
        ).start()
        return carry

    lax.fori_loop(1, 8, row_send, 0)
    pltpu.make_async_copy(refs_ref, ga.at[place], rrow).start()

    eye = (
        lax.broadcasted_iota(jnp.int32, (128, 128), 0) == lax.broadcasted_iota(jnp.int32, (128, 128), 1)
    ).astype(BF16)

    def far_first(t):
        return (z // 4 + jnp.where(t < 2, 1 + 2 * t, 6 - 2 * t)) % 4

    def pass_on(k):
        pltpu.make_async_copy(xr.at[k], xr.at[k], rx.at[k]).wait()
        for x in range(2):
            pulses = xr[k, x].reshape(256, 128)
            flipped = lax.dot_general(eye, pulses, NT, preferred_element_type=F32).astype(BF16)
            for g in range(4):
                for c in range(2):
                    zs[16 * x + 4 * k + g, c] = flipped[32 * g : 32 * g + 32, 128 * c : 128 * c + 128]

        def send(i, carry):
            dest = (i // 4) * 16 + 4 * k + i % 4

            @pl.when(dest != here)
            def _():
                pltpu.make_async_remote_copy(
                    zs.at[dest], turned_ref.at[:, across * 16 + z], sz, rzs,
                    device_id=(dest * 4 + y, sa), device_id_type=MESH,
                ).start()

            @pl.when(dest == here)
            def _():
                pltpu.make_async_copy(zs.at[dest], turned_ref.at[:, across * 16 + z], rzs).start()

            return carry

        lax.fori_loop(0, 8, send, 0)

    @pl.when(is_source)
    def _():
        send_first(0, 0)
        send_first(0, 1)

        def second_half(t, carry):
            @pl.when(sa == 0)
            def _():
                pass_on(far_first(2 * t))
                pass_on(far_first(2 * t + 1))

            @pl.when(t == 0)
            def _():
                pltpu.make_async_copy(hb, hb, rh).wait()
                w1[:, :, REACH - HALO :] = w1[:, :, REACH - HALO :] + hb[...]

            correlate(w1, 1, t)
            send_first(1, t)
            return carry

        lax.fori_loop(0, 2, second_half, 0)

    pltpu.make_async_copy(ga, ga, rrow).wait()
    wanted = jnp.dot(pick_ref[...], ga[...].reshape(128, 512), preferred_element_type=F32)
    for dest in range(16):
        rs[dest] = wanted[2 * dest : 2 * dest + 2].astype(BF16)

    def row_pass(i, carry):
        dest = (z + i) % 16
        pltpu.make_async_remote_copy(
            rs.at[dest], rz.at[z], szrow, rzrow,
            device_id=((xlo * 16 + dest) * 4 + y, sa), device_id_type=MESH,
        ).start()
        return carry

    lax.fori_loop(1, 16, row_pass, 0)
    pltpu.make_async_copy(rs.at[z], rz.at[z], rzrow).start()

    def rest(t, carry):
        pass_on(far_first(t))
        return carry

    lax.fori_loop(jnp.where(sa == 0, 4, 0), 4, rest, 0)

    pltpu.make_async_copy(rz, rz, rzrow).wait()
    row_ref[...] = jnp.sum(rz[...].astype(F32), axis=0)

    pltpu.make_async_copy(turned_ref, turned_ref, rzs).wait()
    pltpu.make_async_copy(zs.at[pl.ds(0, 31)], zs.at[pl.ds(0, 31)], sz).wait()
    pltpu.make_async_copy(rs.at[pl.ds(0, 15)], rs.at[pl.ds(0, 15)], szrow).wait()
    pltpu.make_async_copy(ga.at[pl.ds(0, 7)], ga.at[pl.ds(0, 7)], srow).wait()

    @pl.when(jnp.logical_or(sa == 1, sa == 2))
    def _():
        pltpu.make_async_copy(halo_ref, halo_ref, sh).wait()

    @pl.when(sa == 0)
    def _():
        pltpu.make_async_copy(yb.at[pl.ds(0, 28)], yb.at[pl.ds(0, 28)], sx).wait()

    @pl.when(sa == 1)
    def _():
        pltpu.make_async_copy(yb, yb, sx).wait()


def azimuth_kernel(turned_ref, row_ref, out_ref, lhs, taps, image, sems):
    zeros = jnp.zeros((32, 256), BF16)
    for c in range(2):
        lhs[c, 0] = zeros
        lhs[c, 17] = zeros
        for block in range(16):
            for half in range(2):
                lhs[c, block + 1, :, 128 * half : 128 * half + 128] = turned_ref[c, 2 * block + half]
    for part in range(2):
        row = jnp.concatenate([row_ref[part : part + 1, :], jnp.zeros((1, 512), F32)], axis=1)
        wide = pltpu.roll(jnp.broadcast_to(row, (256, 1024)), 0, 1, stride=1, stride_axis=0)
        taps[256 * part : 256 * part + 256, :] = wide[:, :768].astype(BF16)
    copies = []
    for side in range(2):
        got = []
        for c in range(2):
            total = None
            for o in range(3):
                rows = lhs[c, 8 * side + o : 8 * side + o + 8].reshape(256, 256)
                piece = lax.dot_general(rows, taps[:, 256 * o : 256 * o + 256], NT, preferred_element_type=F32)
                total = piece if total is None else total + piece
            got.append(total)
        real = got[0][:, :256] + got[1][:, 256:]
        imag = got[1][:, :256] - got[0][:, 256:]
        for block in range(8):
            image[side, :, 0, 256 * block : 256 * block + 256] = real[32 * block : 32 * block + 32]
            image[side, :, 1, 256 * block : 256 * block + 256] = imag[32 * block : 32 * block + 32]
        copies.append(
            pltpu.make_async_copy(image.at[side], out_ref.at[:, :, pl.ds(2048 * side, 2048)], sems.at[side])
        )
        copies[-1].start()
    for copy in copies:
        copy.wait()


def params(**more):
    return pltpu.CompilerParams(vmem_limit_bytes=20 << 20, **more)


def on_device(raw_echo, chirp_replica, azimuth_refs, migration_index, window_start):
    large = (migration_index, chirp_replica, raw_echo, azimuth_refs)
    in_hbm = [pltpu.with_memory_space_constraint(value, pltpu.HBM) for value in large]
    dma = pltpu.SemaphoreType.DMA
    turned, row = pl.pallas_call(
        turn_kernel,
        out_shape=(
            jax.ShapeDtypeStruct((2, 32, 32, 128), BF16),
            jax.ShapeDtypeStruct((2, 512), F32),
        ),
        in_specs=[SMEM, HBM, HBM, HBM, HBM],
        out_specs=(ANY, VMEM),
        scratch_shapes=[
            pltpu.VMEM((32, 2, 8192), BF16),
            pltpu.VMEM((2, 32, 8192), BF16),
            pltpu.SMEM((4, 128), jnp.int32),
            pltpu.VMEM((2, 1024), BF16),
            pltpu.VMEM((4, 256, SPAN), BF16),
            pltpu.VMEM((32, 128), BF16),
            pltpu.VMEM((2, 32, REACH), BF16),
            pltpu.VMEM((2, 32, REACH), BF16),
            pltpu.VMEM((2, 32, HALO), BF16),
            pltpu.VMEM((2, 32, HALO), BF16),
            pltpu.VMEM((32, 2, 2, 32, 128), BF16),
            pltpu.VMEM((4, 2, 2, 4, 32, 128), BF16),
            pltpu.VMEM((32, 2, 32, 128), BF16),
            pltpu.VMEM((8, 8, 2, 512), BF16),
            pltpu.VMEM((16, 2, 512), BF16),
            pltpu.VMEM((16, 2, 512), BF16),
            dma((4,)), dma((2,)), dma, dma, dma, dma((4,)), dma, dma, dma, dma, dma, dma,
        ],
        compiler_params=params(collective_id=0, has_side_effects=True),
        name="corner_turn",
    )(window_start, *in_hbm)

    image = pl.pallas_call(
        azimuth_kernel,
        out_shape=jax.ShapeDtypeStruct((32, 2, 4096), F32),
        in_specs=[VMEM, VMEM],
        out_specs=HBM,
        scratch_shapes=[
            pltpu.VMEM((2, 18, 32, 256), BF16),
            pltpu.VMEM((512, 768), BF16),
            pltpu.VMEM((2, 32, 2, 2048), F32),
            dma((2,)),
        ],
        compiler_params=params(),
        name="azimuth_correlate",
    )(turned, row)
    return image[None]


def solution(mesh):
    placed = (P("pa", None, "sa"), P(), P("pa", None, None), P(), P())
    return jax.shard_map(
        on_device, mesh=mesh, in_specs=placed, out_specs=P("sa", "pa", None, None), check_vma=False
    )
```

```python
import functools

import jax
import jax.numpy as jnp
from jax import lax
from jax.experimental import pallas as pl
from jax.experimental.pallas import tpu as pltpu
from jax.sharding import PartitionSpec as P

MESH = pl.DeviceIdType.MESH
BF16 = jnp.bfloat16
F32 = jnp.float32
NT = (((1,), (1,)), ((), ()))
SPAN = 1664
HALO = 3072
REACH = 5248
VMEM = pl.BlockSpec(memory_space=pltpu.VMEM)
SMEM = pl.BlockSpec(memory_space=pltpu.SMEM)
ANY = pl.BlockSpec(memory_space=pl.ANY)
HBM = pl.BlockSpec(memory_space=pltpu.HBM)


def turn_kernel(
    start_ref, index_hbm, chirp_hbm, raw_hbm, refs_ref, turned_ref, row_ref,
    raw_ref, planar_ref, index_ref, chirp_ref, taps_ref, pick_ref, w0, w1, halo_ref, hb, yb, xr, zs, ga, rs, rz, sraw, sin, sh, rh, sx, rx, sz, rzs, srow, rrow, szrow, rzrow,
):
    pa = lax.axis_index("pa")
    sa = lax.axis_index("sa")
    xlo, z, y = pa // 64, (pa // 4) % 16, pa % 4
    xhi, core = sa // 2, sa % 2
    here = xlo * 16 + z
    across = jnp.where(xhi == 0, xlo, 1 - xlo)
    is_source = xhi == 0
    place = xlo * 4 + y

    get_index = pltpu.make_async_copy(index_hbm, index_ref, sin.at[0])
    get_chirp = pltpu.make_async_copy(chirp_hbm, chirp_ref, sin.at[1])
    get_chirp.start()
    get_index.start()

    def get_raw(q):
        part = pl.ds(2048 * q, 2048)
        return pltpu.make_async_copy(raw_hbm.at[:, :, part], raw_ref.at[:, :, part], sraw.at[q])

    for q in range(4):
        get_raw(q).start()

    barrier = pltpu.get_barrier_semaphore()

    @pl.when(sa != 0)
    def _():
        def greet_source(i, carry):
            dev = (across * 16 + z) * 4 + i
            pl.semaphore_signal(barrier, inc=1, device_id=(dev, xhi), device_id_type=MESH)
            return carry

        lax.fori_loop(0, 4, greet_source, 0)

    def greet_plane(i, carry):
        dev = ((i // 3) * 16 + z) * 4 + (y + 1 + i % 3) % 4
        pl.semaphore_signal(barrier, inc=1, device_id=(dev, sa), device_id_type=MESH)
        return carry

    lax.fori_loop(0, 6, greet_plane, 0)

    def greet_line(i, carry):
        dev = ((here + i) % 32) * 4 + y
        pl.semaphore_signal(barrier, inc=1, device_id=(dev, sa), device_id_type=MESH)
        return carry

    lax.fori_loop(1, 32, greet_line, 0)

    @pl.when(sa < 2)
    def _():
        pl.semaphore_signal(barrier, inc=1, device_id=(pa, sa + 1), device_id_type=MESH)

    start = start_ref[0]
    bits = [jnp.bitwise_and(lax.shift_right_logical(start, bit), 1) == 1 for bit in range(11)]

    def shifted(value):
        for bit in (10, 9, 8, 7):
            step = 1 << bit
            value = jnp.where(bits[bit], value[:, step:], value[:, : value.shape[1] - step])
        return value

    get_chirp.wait()

    @pl.when(is_source)
    def _():
        for part in range(2):
            row = jnp.concatenate([chirp_ref[part : part + 1, :].astype(F32), jnp.zeros((1, 256), F32)], axis=1)
            row = jnp.broadcast_to(row, (8, 1280))
            for bit in range(7):
                row = jnp.where(bits[bit], pltpu.roll(row, 1 << bit, 1), row)
            wide = pltpu.roll(jnp.broadcast_to(row[:1], (128, 1280)), 0, 1, stride=1, stride_axis=0)
            wide = wide.astype(BF16)
            for dest in range(4):
                for g in range(4):
                    r0 = part * 128 + g * 32
                    if g > 0:
                        taps_ref[dest, r0 : r0 + 32, : 128 * g] = jnp.zeros((32, 128 * g), BF16)
                    taps_ref[dest, r0 : r0 + 32, 128 * g : 128 * g + 1280] = wide[32 * dest : 32 * dest + 32, :]
                    if g < 3:
                        taps_ref[dest, r0 : r0 + 32, 128 * g + 1280 :] = jnp.zeros((32, 384 - 128 * g), BF16)

    get_index.wait()
    entry = lax.broadcasted_iota(jnp.int32, (32, 128), 0)
    code = jnp.full((32, 128), -2, jnp.int32)
    for dest in range(16):
        index = index_ref[sa, xlo * 64 + 4 * dest + y]
        slot = (index // 512) * 32 + index % 32
        code = jnp.where(entry // 2 == dest, jnp.where((index // 32) % 16 == z, 2 * slot, -2), code)
    pick_ref[...] = (lax.broadcasted_iota(jnp.int32, (32, 128), 1) == code + entry % 2).astype(F32).astype(BF16)

    source_row = lax.broadcasted_iota(jnp.int32, (64, 64), 1)
    target_row = lax.broadcasted_iota(jnp.int32, (64, 64), 0)
    apart = (source_row == 2 * (target_row % 32) + target_row // 32).astype(F32).astype(BF16)
    for q in range(4):
        get_raw(q).wait()
        rows = raw_ref[:, :, 2048 * q : 2048 * q + 2048].reshape(64, 2048)
        rows = jnp.dot(apart, rows, preferred_element_type=F32).astype(BF16)
        planar_ref[0, :, 2048 * q : 2048 * q + 2048] = rows[:32]
        planar_ref[1, :, 2048 * q : 2048 * q + 2048] = rows[32:]

    @pl.when(jnp.logical_or(sa == 1, sa == 2))
    def _():
        for c in range(2):
            for r0 in (0, 16):
                head = jnp.concatenate([jnp.zeros((16, 1920), BF16), planar_ref[c, r0 : r0 + 16, :HALO]], axis=1)
                halo_ref[c, r0 : r0 + 16, :] = shifted(head)

    def correlate(window, jj, t):
        first = (z // 4 + t + 1) % 2
        pieces = []
        for c in range(2):
            for kk in range(2):
                for x in range(2):
                    off = pl.multiple_of(x * 2048 + (first + 2 * kk) * 512, 128)
                    pieces.append(window[c, :, pl.ds(off, SPAN)])
        lhs = jnp.concatenate(pieces, axis=0)
        for dest in range(4):
            got = lax.dot_general(lhs, taps_ref[dest], NT, preferred_element_type=F32)
            real = (got[:128, :128] + got[128:, 128:]).astype(BF16)
            imag = (got[128:, :128] - got[:128, 128:]).astype(BF16)
            for kk in range(2):
                slot = (jj * 4 + first + 2 * kk) * 4 + dest
                for x in range(2):
                    r0 = 64 * kk + 32 * x
                    yb[slot, x, 0] = real[r0 : r0 + 32]
                    yb[slot, x, 1] = imag[r0 : r0 + 32]

    def send_first(jj, t):
        first = (z // 4 + t + 1) % 2

        def send(i, carry):
            k, dest = first + 2 * (i // 4), (y + i) % 4
            dev = ((jnp.where(core == 0, xlo, 1 - xlo)) * 16 + z) * 4 + dest
            target = 2 * core + jj
            there = jnp.logical_or(dev != pa, target != sa)
            slot = (jj * 4 + k) * 4 + dest

            @pl.when(there)
            def _():
                pltpu.make_async_remote_copy(
                    yb.at[slot], xr.at[k, y], sx, rx.at[k],
                    device_id=(dev, target), device_id_type=MESH,
                ).start()

            @pl.when(jnp.logical_not(there))
            def _():
                pltpu.make_async_copy(yb.at[slot], xr.at[k, y], rx.at[k]).start()

            return carry

        lax.fori_loop(0, 8, send, 0)

    @pl.when(is_source)
    def _():
        for c in range(2):
            for r0 in (0, 16):
                w0[c, r0 : r0 + 16, :] = shifted(planar_ref[c, r0 : r0 + 16, :7168])

        def first_half(t, carry):
            correlate(w0, 0, t)
            return carry

        lax.fori_loop(0, 2, first_half, 0)
        for c in range(2):
            for r0 in (0, 16):
                tail = jnp.concatenate([planar_ref[c, r0 : r0 + 16, 4096:], jnp.zeros((16, HALO), BF16)], axis=1)
                w1[c, r0 : r0 + 16, :] = shifted(tail)

    @pl.when(sa == 0)
    def _():
        pl.semaphore_wait(barrier, 41)

    @pl.when(sa == 1)
    def _():
        pl.semaphore_wait(barrier, 46)

    @pl.when(sa == 2)
    def _():
        pl.semaphore_wait(barrier, 38)

    @pl.when(sa == 3)
    def _():
        pl.semaphore_wait(barrier, 37)

    @pl.when(jnp.logical_or(sa == 1, sa == 2))
    def _():
        pltpu.make_async_remote_copy(
            halo_ref, hb, sh, rh,
            device_id=(pa, sa - 1), device_id_type=MESH,
        ).start()

    def row_send(i, carry):
        there = (place + i) % 8
        pltpu.make_async_remote_copy(
            refs_ref, ga.at[place], srow, rrow,
            device_id=(((there // 4) * 16 + z) * 4 + there % 4, sa), device_id_type=MESH,
        ).start()
        return carry

    lax.fori_loop(1, 8, row_send, 0)
    pltpu.make_async_copy(refs_ref, ga.at[place], rrow).start()

    eye = (
        lax.broadcasted_iota(jnp.int32, (128, 128), 0) == lax.broadcasted_iota(jnp.int32, (128, 128), 1)
    ).astype(BF16)

    def far_first(t):
        return (z // 4 + jnp.where(t < 2, 1 + 2 * t, 6 - 2 * t)) % 4

    def pass_on(k):
        pltpu.make_async_copy(xr.at[k], xr.at[k], rx.at[k]).wait()
        for x in range(2):
            pulses = jnp.concatenate([xr[k, :, x, c].reshape(128, 128) for c in range(2)], axis=0)
            flipped = lax.dot_general(eye, pulses, NT, preferred_element_type=F32).astype(BF16)
            for g in range(4):
                for c in range(2):
                    zs[16 * x + 4 * k + g, c] = flipped[32 * g : 32 * g + 32, 128 * c : 128 * c + 128]

        def send(i, carry):
            dest = (i // 4) * 16 + 4 * k + i % 4

            @pl.when(dest != here)
            def _():
                pltpu.make_async_remote_copy(
                    zs.at[dest], turned_ref.at[across * 16 + z], sz, rzs,
                    device_id=(dest * 4 + y, sa), device_id_type=MESH,
                ).start()

            @pl.when(dest == here)
            def _():
                pltpu.make_async_copy(zs.at[dest], turned_ref.at[across * 16 + z], rzs).start()

            return carry

        lax.fori_loop(0, 8, send, 0)

    @pl.when(is_source)
    def _():
        send_first(0, 0)
        send_first(0, 1)

        def second_half(t, carry):
            @pl.when(sa == 0)
            def _():
                pass_on(far_first(2 * t))
                pass_on(far_first(2 * t + 1))

            @pl.when(t == 0)
            def _():
                pltpu.make_async_copy(hb, hb, rh).wait()
                w1[:, :, REACH - HALO :] = w1[:, :, REACH - HALO :] + hb[...]

            correlate(w1, 1, t)
            send_first(1, t)
            return carry

        lax.fori_loop(0, 2, second_half, 0)

    def rest(t, carry):
        pass_on(far_first(t))
        return carry

    lax.fori_loop(jnp.where(sa == 0, 2, 0), 2, rest, 0)

    pltpu.make_async_copy(ga, ga, rrow).wait()
    wanted = jnp.dot(pick_ref[...], ga[...].reshape(128, 512), preferred_element_type=F32)
    for dest in range(16):
        rs[dest] = wanted[2 * dest : 2 * dest + 2].astype(BF16)

    def row_pass(i, carry):
        dest = (z + i) % 16
        pltpu.make_async_remote_copy(
            rs.at[dest], rz.at[z], szrow, rzrow,
            device_id=((xlo * 16 + dest) * 4 + y, sa), device_id_type=MESH,
        ).start()
        return carry

    lax.fori_loop(1, 16, row_pass, 0)
    pltpu.make_async_copy(rs.at[z], rz.at[z], rzrow).start()

    lax.fori_loop(jnp.where(sa == 0, 4, 2), 4, rest, 0)

    pltpu.make_async_copy(rz, rz, rzrow).wait()
    row_ref[...] = jnp.sum(rz[...].astype(F32), axis=0)

    pltpu.make_async_copy(turned_ref, turned_ref, rzs).wait()
    pltpu.make_async_copy(zs.at[pl.ds(0, 31)], zs.at[pl.ds(0, 31)], sz).wait()
    pltpu.make_async_copy(rs.at[pl.ds(0, 15)], rs.at[pl.ds(0, 15)], szrow).wait()
    pltpu.make_async_copy(ga.at[pl.ds(0, 7)], ga.at[pl.ds(0, 7)], srow).wait()

    @pl.when(jnp.logical_or(sa == 1, sa == 2))
    def _():
        pltpu.make_async_copy(halo_ref, halo_ref, sh).wait()

    @pl.when(sa == 0)
    def _():
        pltpu.make_async_copy(yb.at[pl.ds(0, 28)], yb.at[pl.ds(0, 28)], sx).wait()

    @pl.when(sa == 1)
    def _():
        pltpu.make_async_copy(yb, yb, sx).wait()


def azimuth_kernel(turned_ref, row_ref, out_ref, lhs, taps, image, sems):
    zeros = jnp.zeros((32, 256), BF16)
    for c in range(2):
        lhs[c, 0] = zeros
        lhs[c, 17] = zeros
        for block in range(16):
            for half in range(2):
                lhs[c, block + 1, :, 128 * half : 128 * half + 128] = turned_ref[2 * block + half, c]
    for part in range(2):
        row = jnp.concatenate([row_ref[part : part + 1, :], jnp.zeros((1, 512), F32)], axis=1)
        wide = pltpu.roll(jnp.broadcast_to(row, (256, 1024)), 0, 1, stride=1, stride_axis=0)
        taps[256 * part : 256 * part + 256, :] = wide[:, :768].astype(BF16)
    copies = []
    for side in range(2):
        got = []
        for c in range(2):
            total = None
            for o in range(3):
                rows = lhs[c, 8 * side + o : 8 * side + o + 8].reshape(256, 256)
                piece = lax.dot_general(rows, taps[:, 256 * o : 256 * o + 256], NT, preferred_element_type=F32)
                total = piece if total is None else total + piece
            got.append(total)
        real = got[0][:, :256] + got[1][:, 256:]
        imag = got[1][:, :256] - got[0][:, 256:]
        for block in range(8):
            image[side, :, 0, 256 * block : 256 * block + 256] = real[32 * block : 32 * block + 32]
            image[side, :, 1, 256 * block : 256 * block + 256] = imag[32 * block : 32 * block + 32]
        copies.append(
            pltpu.make_async_copy(image.at[side], out_ref.at[:, :, pl.ds(2048 * side, 2048)], sems.at[side])
        )
        copies[-1].start()
    for copy in copies:
        copy.wait()


def params(**more):
    return pltpu.CompilerParams(vmem_limit_bytes=20 << 20, **more)


def on_device(raw_echo, chirp_replica, azimuth_refs, migration_index, window_start):
    large = (migration_index, chirp_replica, raw_echo, azimuth_refs)
    in_hbm = [pltpu.with_memory_space_constraint(value, pltpu.HBM) for value in large]
    dma = pltpu.SemaphoreType.DMA
    turned, row = pl.pallas_call(
        turn_kernel,
        out_shape=(
            jax.ShapeDtypeStruct((32, 2, 32, 128), BF16),
            jax.ShapeDtypeStruct((2, 512), F32),
        ),
        in_specs=[SMEM, HBM, HBM, HBM, HBM],
        out_specs=(ANY, VMEM),
        scratch_shapes=[
            pltpu.VMEM((32, 2, 8192), BF16),
            pltpu.VMEM((2, 32, 8192), BF16),
            pltpu.SMEM((4, 128), jnp.int32),
            pltpu.VMEM((2, 1024), BF16),
            pltpu.VMEM((4, 256, SPAN), BF16),
            pltpu.VMEM((32, 128), BF16),
            pltpu.VMEM((2, 32, REACH), BF16),
            pltpu.VMEM((2, 32, REACH), BF16),
            pltpu.VMEM((2, 32, HALO), BF16),
            pltpu.VMEM((2, 32, HALO), BF16),
            pltpu.VMEM((32, 2, 2, 32, 128), BF16),
            pltpu.VMEM((4, 4, 2, 2, 32, 128), BF16),
            pltpu.VMEM((32, 2, 32, 128), BF16),
            pltpu.VMEM((8, 8, 2, 512), BF16),
            pltpu.VMEM((16, 2, 512), BF16),
            pltpu.VMEM((16, 2, 512), BF16),
            dma((4,)), dma((2,)), dma, dma, dma, dma((4,)), dma, dma, dma, dma, dma, dma,
        ],
        compiler_params=params(collective_id=0, has_side_effects=True),
        name="corner_turn",
    )(window_start, *in_hbm)

    image = pl.pallas_call(
        azimuth_kernel,
        out_shape=jax.ShapeDtypeStruct((32, 2, 4096), F32),
        in_specs=[VMEM, VMEM],
        out_specs=HBM,
        scratch_shapes=[
            pltpu.VMEM((2, 18, 32, 256), BF16),
            pltpu.VMEM((512, 768), BF16),
            pltpu.VMEM((2, 32, 2, 2048), F32),
            dma((2,)),
        ],
        compiler_params=params(),
        name="azimuth_correlate",
    )(turned, row)
    return image[None]


def solution(mesh):
    placed = (P("pa", None, "sa"), P(), P("pa", None, None), P(), P())
    return jax.shard_map(
        on_device, mesh=mesh, in_specs=placed, out_specs=P("sa", "pa", None, None), check_vma=False
    )
```

```python
import functools

import jax
import jax.numpy as jnp
from jax import lax
from jax.experimental import pallas as pl
from jax.experimental.pallas import tpu as pltpu
from jax.sharding import PartitionSpec as P

MESH = pl.DeviceIdType.MESH
BF16 = jnp.bfloat16
F32 = jnp.float32
NT = (((1,), (1,)), ((), ()))
SPAN = 1664
HALO = 3072
REACH = 5248
VMEM = pl.BlockSpec(memory_space=pltpu.VMEM)
SMEM = pl.BlockSpec(memory_space=pltpu.SMEM)
ANY = pl.BlockSpec(memory_space=pl.ANY)
HBM = pl.BlockSpec(memory_space=pltpu.HBM)


def turn_kernel(
    start_ref, index_hbm, chirp_hbm, raw_hbm, refs_ref, turned_ref, row_ref,
    raw_ref, planar_ref, index_ref, chirp_ref, taps_ref, pick_ref, w0, w1, halo_ref, hb, yb, xr, zs, ga, rs, rz, sraw, sin, sh, rh, sx, rx, sz, rzs, srow, rrow, szrow, rzrow,
):
    pa = lax.axis_index("pa")
    sa = lax.axis_index("sa")
    xlo, z, y = pa // 64, (pa // 4) % 16, pa % 4
    xhi, core = sa // 2, sa % 2
    here = xlo * 16 + z
    across = jnp.where(xhi == 0, xlo, 1 - xlo)
    is_source = xhi == 0
    place = xlo * 4 + y

    get_index = pltpu.make_async_copy(index_hbm, index_ref, sin.at[0])
    get_chirp = pltpu.make_async_copy(chirp_hbm, chirp_ref, sin.at[1])
    get_chirp.start()
    get_index.start()

    def get_raw(q):
        part = pl.ds(2048 * q, 2048)
        return pltpu.make_async_copy(raw_hbm.at[:, :, part], raw_ref.at[:, :, part], sraw.at[q])

    for q in range(4):
        get_raw(q).start()

    barrier = pltpu.get_barrier_semaphore()

    @pl.when(sa != 0)
    def _():
        def greet_source(i, carry):
            dev = (across * 16 + z) * 4 + i
            pl.semaphore_signal(barrier, inc=1, device_id=(dev, xhi), device_id_type=MESH)
            return carry

        lax.fori_loop(0, 4, greet_source, 0)

    def greet_plane(i, carry):
        dev = ((i // 3) * 16 + z) * 4 + (y + 1 + i % 3) % 4
        pl.semaphore_signal(barrier, inc=1, device_id=(dev, sa), device_id_type=MESH)
        return carry

    lax.fori_loop(0, 6, greet_plane, 0)

    def greet_line(i, carry):
        dev = ((here + i) % 32) * 4 + y
        pl.semaphore_signal(barrier, inc=1, device_id=(dev, sa), device_id_type=MESH)
        return carry

    lax.fori_loop(1, 32, greet_line, 0)

    @pl.when(sa < 2)
    def _():
        pl.semaphore_signal(barrier, inc=1, device_id=(pa, sa + 1), device_id_type=MESH)

    start = start_ref[0]
    bits = [jnp.bitwise_and(lax.shift_right_logical(start, bit), 1) == 1 for bit in range(11)]

    def shifted(value):
        for bit in (10, 9, 8, 7):
            step = 1 << bit
            value = jnp.where(bits[bit], value[:, step:], value[:, : value.shape[1] - step])
        return value

    get_chirp.wait()

    @pl.when(is_source)
    def _():
        for part in range(2):
            row = jnp.concatenate([chirp_ref[part : part + 1, :].astype(F32), jnp.zeros((1, 256), F32)], axis=1)
            row = jnp.broadcast_to(row, (8, 1280))
            for bit in range(7):
                row = jnp.where(bits[bit], pltpu.roll(row, 1 << bit, 1), row)
            wide = pltpu.roll(jnp.broadcast_to(row[:1], (128, 1280)), 0, 1, stride=1, stride_axis=0)
            wide = wide.astype(BF16)
            for dest in range(4):
                for g in range(4):
                    r0 = part * 128 + g * 32
                    if g > 0:
                        taps_ref[dest, r0 : r0 + 32, : 128 * g] = jnp.zeros((32, 128 * g), BF16)
                    taps_ref[dest, r0 : r0 + 32, 128 * g : 128 * g + 1280] = wide[32 * dest : 32 * dest + 32, :]
                    if g < 3:
                        taps_ref[dest, r0 : r0 + 32, 128 * g + 1280 :] = jnp.zeros((32, 384 - 128 * g), BF16)

    get_index.wait()
    entry = lax.broadcasted_iota(jnp.int32, (32, 128), 0)
    code = jnp.full((32, 128), -2, jnp.int32)
    for dest in range(16):
        index = index_ref[sa, xlo * 64 + 4 * dest + y]
        slot = (index // 512) * 32 + index % 32
        code = jnp.where(entry // 2 == dest, jnp.where((index // 32) % 16 == z, 2 * slot, -2), code)
    pick_ref[...] = (lax.broadcasted_iota(jnp.int32, (32, 128), 1) == code + entry % 2).astype(F32).astype(BF16)

    source_row = lax.broadcasted_iota(jnp.int32, (64, 64), 1)
    target_row = lax.broadcasted_iota(jnp.int32, (64, 64), 0)
    apart = (source_row == 2 * (target_row % 32) + target_row // 32).astype(F32).astype(BF16)
    for q in range(4):
        get_raw(q).wait()
        rows = raw_ref[:, :, 2048 * q : 2048 * q + 2048].reshape(64, 2048)
        rows = jnp.dot(apart, rows, preferred_element_type=F32).astype(BF16)
        planar_ref[0, :, 2048 * q : 2048 * q + 2048] = rows[:32]
        planar_ref[1, :, 2048 * q : 2048 * q + 2048] = rows[32:]

    @pl.when(jnp.logical_or(sa == 1, sa == 2))
    def _():
        for c in range(2):
            for r0 in (0, 16):
                head = jnp.concatenate([jnp.zeros((16, 1920), BF16), planar_ref[c, r0 : r0 + 16, :HALO]], axis=1)
                halo_ref[c, r0 : r0 + 16, :] = shifted(head)

    def correlate(window, jj, t):
        first = (z // 4 + t + 1) % 2
        pieces = []
        for c in range(2):
            for kk in range(2):
                for x in range(2):
                    off = pl.multiple_of(x * 2048 + (first + 2 * kk) * 512, 128)
                    pieces.append(window[c, :, pl.ds(off, SPAN)])
        lhs = jnp.concatenate(pieces, axis=0)
        for dest in range(4):
            got = lax.dot_general(lhs, taps_ref[dest], NT, preferred_element_type=F32)
            real = (got[:128, :128] + got[128:, 128:]).astype(BF16)
            imag = (got[128:, :128] - got[:128, 128:]).astype(BF16)
            for kk in range(2):
                slot = (jj * 4 + first + 2 * kk) * 4 + dest
                for x in range(2):
                    r0 = 64 * kk + 32 * x
                    yb[slot, x, 0] = real[r0 : r0 + 32]
                    yb[slot, x, 1] = imag[r0 : r0 + 32]

    def send_first(jj, t):
        first = (z // 4 + t + 1) % 2

        def send(i, carry):
            k, dest = first + 2 * (i // 4), (y + i) % 4
            dev = ((jnp.where(core == 0, xlo, 1 - xlo)) * 16 + z) * 4 + dest
            target = 2 * core + jj
            there = jnp.logical_or(dev != pa, target != sa)
            slot = (jj * 4 + k) * 4 + dest

            @pl.when(there)
            def _():
                pltpu.make_async_remote_copy(
                    yb.at[slot], xr.at[k, y], sx, rx.at[k],
                    device_id=(dev, target), device_id_type=MESH,
                ).start()

            @pl.when(jnp.logical_not(there))
            def _():
                pltpu.make_async_copy(yb.at[slot], xr.at[k, y], rx.at[k]).start()

            return carry

        lax.fori_loop(0, 8, send, 0)

    @pl.when(is_source)
    def _():
        for c in range(2):
            for r0 in (0, 16):
                w0[c, r0 : r0 + 16, :] = shifted(planar_ref[c, r0 : r0 + 16, :7168])

        def first_half(t, carry):
            correlate(w0, 0, t)
            return carry

        lax.fori_loop(0, 2, first_half, 0)
        for c in range(2):
            for r0 in (0, 16):
                tail = jnp.concatenate([planar_ref[c, r0 : r0 + 16, 4096:], jnp.zeros((16, HALO), BF16)], axis=1)
                w1[c, r0 : r0 + 16, :] = shifted(tail)

    @pl.when(sa == 0)
    def _():
        pl.semaphore_wait(barrier, 41)

    @pl.when(sa == 1)
    def _():
        pl.semaphore_wait(barrier, 46)

    @pl.when(sa == 2)
    def _():
        pl.semaphore_wait(barrier, 38)

    @pl.when(sa == 3)
    def _():
        pl.semaphore_wait(barrier, 37)

    @pl.when(jnp.logical_or(sa == 1, sa == 2))
    def _():
        for c in range(2):
            for r0 in (0, 16):
                piece = (c, pl.ds(r0, 16))
                pltpu.make_async_remote_copy(
                    halo_ref.at[piece], hb.at[piece], sh, rh,
                    device_id=(pa, sa - 1), device_id_type=MESH,
                ).start()

    def row_send(i, carry):
        there = (place + i) % 8
        pltpu.make_async_remote_copy(
            refs_ref, ga.at[place], srow, rrow,
            device_id=(((there // 4) * 16 + z) * 4 + there % 4, sa), device_id_type=MESH,
        ).start()
        return carry

    lax.fori_loop(1, 8, row_send, 0)
    pltpu.make_async_copy(refs_ref, ga.at[place], rrow).start()

    eye = (
        lax.broadcasted_iota(jnp.int32, (128, 128), 0) == lax.broadcasted_iota(jnp.int32, (128, 128), 1)
    ).astype(BF16)

    def far_first(t):
        return (z // 4 + jnp.where(t < 2, 1 + 2 * t, 6 - 2 * t)) % 4

    def pass_on(k):
        pltpu.make_async_copy(xr.at[k], xr.at[k], rx.at[k]).wait()
        for x in range(2):
            pulses = jnp.concatenate([xr[k, :, x, c].reshape(128, 128) for c in range(2)], axis=0)
            flipped = lax.dot_general(eye, pulses, NT, preferred_element_type=F32).astype(BF16)
            for g in range(4):
                for c in range(2):
                    zs[16 * x + 4 * k + g, c] = flipped[32 * g : 32 * g + 32, 128 * c : 128 * c + 128]

        def send(i, carry):
            dest = (i // 4) * 16 + 4 * k + i % 4

            @pl.when(dest != here)
            def _():
                pltpu.make_async_remote_copy(
                    zs.at[dest], turned_ref.at[across * 16 + z], sz, rzs,
                    device_id=(dest * 4 + y, sa), device_id_type=MESH,
                ).start()

            @pl.when(dest == here)
            def _():
                pltpu.make_async_copy(zs.at[dest], turned_ref.at[across * 16 + z], rzs).start()

            return carry

        lax.fori_loop(0, 8, send, 0)

    @pl.when(is_source)
    def _():
        send_first(0, 0)
        send_first(0, 1)

        def second_half(t, carry):
            @pl.when(sa == 0)
            def _():
                pass_on(far_first(2 * t))
                pass_on(far_first(2 * t + 1))

            @pl.when(t == 0)
            def _():
                pltpu.make_async_copy(hb, hb, rh).wait()
                w1[:, :, REACH - HALO :] = w1[:, :, REACH - HALO :] + hb[...]

            correlate(w1, 1, t)
            send_first(1, t)
            return carry

        lax.fori_loop(0, 2, second_half, 0)

    def rest(t, carry):
        pass_on(far_first(t))
        return carry

    lax.fori_loop(jnp.where(sa == 0, 2, 0), 2, rest, 0)

    pltpu.make_async_copy(ga, ga, rrow).wait()
    wanted = jnp.dot(pick_ref[...], ga[...].reshape(128, 512), preferred_element_type=F32)
    for dest in range(16):
        rs[dest] = wanted[2 * dest : 2 * dest + 2].astype(BF16)

    def row_pass(i, carry):
        dest = (z + i) % 16
        pltpu.make_async_remote_copy(
            rs.at[dest], rz.at[z], szrow, rzrow,
            device_id=((xlo * 16 + dest) * 4 + y, sa), device_id_type=MESH,
        ).start()
        return carry

    lax.fori_loop(1, 16, row_pass, 0)
    pltpu.make_async_copy(rs.at[z], rz.at[z], rzrow).start()

    lax.fori_loop(jnp.where(sa == 0, 4, 2), 4, rest, 0)

    pltpu.make_async_copy(rz, rz, rzrow).wait()
    row_ref[...] = jnp.sum(rz[...].astype(F32), axis=0)

    pltpu.make_async_copy(turned_ref, turned_ref, rzs).wait()
    pltpu.make_async_copy(zs.at[pl.ds(0, 31)], zs.at[pl.ds(0, 31)], sz).wait()
    pltpu.make_async_copy(rs.at[pl.ds(0, 15)], rs.at[pl.ds(0, 15)], szrow).wait()
    pltpu.make_async_copy(ga.at[pl.ds(0, 7)], ga.at[pl.ds(0, 7)], srow).wait()

    @pl.when(jnp.logical_or(sa == 1, sa == 2))
    def _():
        pltpu.make_async_copy(halo_ref, halo_ref, sh).wait()

    @pl.when(sa == 0)
    def _():
        pltpu.make_async_copy(yb.at[pl.ds(0, 28)], yb.at[pl.ds(0, 28)], sx).wait()

    @pl.when(sa == 1)
    def _():
        pltpu.make_async_copy(yb, yb, sx).wait()


def azimuth_kernel(turned_ref, row_ref, out_ref, lhs, taps, image, sems):
    zeros = jnp.zeros((32, 256), BF16)
    for c in range(2):
        lhs[c, 0] = zeros
        lhs[c, 17] = zeros
        for block in range(16):
            for half in range(2):
                lhs[c, block + 1, :, 128 * half : 128 * half + 128] = turned_ref[2 * block + half, c]
    for part in range(2):
        row = jnp.concatenate([row_ref[part : part + 1, :], jnp.zeros((1, 512), F32)], axis=1)
        wide = pltpu.roll(jnp.broadcast_to(row, (256, 1024)), 0, 1, stride=1, stride_axis=0)
        taps[256 * part : 256 * part + 256, :] = wide[:, :768].astype(BF16)
    copies = []
    for side in range(2):
        got = []
        for c in range(2):
            total = None
            for o in range(3):
                rows = lhs[c, 8 * side + o : 8 * side + o + 8].reshape(256, 256)
                piece = lax.dot_general(rows, taps[:, 256 * o : 256 * o + 256], NT, preferred_element_type=F32)
                total = piece if total is None else total + piece
            got.append(total)
        real = got[0][:, :256] + got[1][:, 256:]
        imag = got[1][:, :256] - got[0][:, 256:]
        for block in range(8):
            image[side, :, 0, 256 * block : 256 * block + 256] = real[32 * block : 32 * block + 32]
            image[side, :, 1, 256 * block : 256 * block + 256] = imag[32 * block : 32 * block + 32]
        copies.append(
            pltpu.make_async_copy(image.at[side], out_ref.at[:, :, pl.ds(2048 * side, 2048)], sems.at[side])
        )
        copies[-1].start()
    for copy in copies:
        copy.wait()


def params(**more):
    return pltpu.CompilerParams(vmem_limit_bytes=20 << 20, **more)


def on_device(raw_echo, chirp_replica, azimuth_refs, migration_index, window_start):
    large = (migration_index, chirp_replica, raw_echo, azimuth_refs)
    in_hbm = [pltpu.with_memory_space_constraint(value, pltpu.HBM) for value in large]
    dma = pltpu.SemaphoreType.DMA
    turned, row = pl.pallas_call(
        turn_kernel,
        out_shape=(
            jax.ShapeDtypeStruct((32, 2, 32, 128), BF16),
            jax.ShapeDtypeStruct((2, 512), F32),
        ),
        in_specs=[SMEM, HBM, HBM, HBM, HBM],
        out_specs=(ANY, VMEM),
        scratch_shapes=[
            pltpu.VMEM((32, 2, 8192), BF16),
            pltpu.VMEM((2, 32, 8192), BF16),
            pltpu.SMEM((4, 128), jnp.int32),
            pltpu.VMEM((2, 1024), BF16),
            pltpu.VMEM((4, 256, SPAN), BF16),
            pltpu.VMEM((32, 128), BF16),
            pltpu.VMEM((2, 32, REACH), BF16),
            pltpu.VMEM((2, 32, REACH), BF16),
            pltpu.VMEM((2, 32, HALO), BF16),
            pltpu.VMEM((2, 32, HALO), BF16),
            pltpu.VMEM((32, 2, 2, 32, 128), BF16),
            pltpu.VMEM((4, 4, 2, 2, 32, 128), BF16),
            pltpu.VMEM((32, 2, 32, 128), BF16),
            pltpu.VMEM((8, 8, 2, 512), BF16),
            pltpu.VMEM((16, 2, 512), BF16),
            pltpu.VMEM((16, 2, 512), BF16),
            dma((4,)), dma((2,)), dma, dma, dma, dma((4,)), dma, dma, dma, dma, dma, dma,
        ],
        compiler_params=params(collective_id=0, has_side_effects=True),
        name="corner_turn",
    )(window_start, *in_hbm)

    image = pl.pallas_call(
        azimuth_kernel,
        out_shape=jax.ShapeDtypeStruct((32, 2, 4096), F32),
        in_specs=[VMEM, VMEM],
        out_specs=HBM,
        scratch_shapes=[
            pltpu.VMEM((2, 18, 32, 256), BF16),
            pltpu.VMEM((512, 768), BF16),
            pltpu.VMEM((2, 32, 2, 2048), F32),
            dma((2,)),
        ],
        compiler_params=params(),
        name="azimuth_correlate",
    )(turned, row)
    return image[None]


def solution(mesh):
    placed = (P("pa", None, "sa"), P(), P("pa", None, None), P(), P())
    return jax.shard_map(
        on_device, mesh=mesh, in_specs=placed, out_specs=P("sa", "pa", None, None), check_vma=False
    )
```

```python
import functools

import jax
import jax.numpy as jnp
from jax import lax
from jax.experimental import pallas as pl
from jax.experimental.pallas import tpu as pltpu
from jax.sharding import PartitionSpec as P

MESH = pl.DeviceIdType.MESH
BF16 = jnp.bfloat16
F32 = jnp.float32
NT = (((1,), (1,)), ((), ()))
SPAN = 1664
HALO = 3072
REACH = 5248
VMEM = pl.BlockSpec(memory_space=pltpu.VMEM)
SMEM = pl.BlockSpec(memory_space=pltpu.SMEM)
ANY = pl.BlockSpec(memory_space=pl.ANY)
HBM = pl.BlockSpec(memory_space=pltpu.HBM)


def turn_kernel(
    start_ref, index_hbm, chirp_hbm, raw_hbm, refs_ref, turned_ref, row_ref,
    raw_ref, planar_ref, index_ref, chirp_ref, taps_ref, pick_ref, w0, w1, halo_ref, hb, yb, xr, zs, ga, rs, rz, sraw, sin, sh, rh, sx, rx, sz, rzs, srow, rrow, szrow, rzrow,
):
    pa = lax.axis_index("pa")
    sa = lax.axis_index("sa")
    xlo, z, y = pa // 64, (pa // 4) % 16, pa % 4
    xhi, core = sa // 2, sa % 2
    here = xlo * 16 + z
    across = jnp.where(xhi == 0, xlo, 1 - xlo)
    is_source = xhi == 0
    place = xlo * 4 + y

    barrier = pltpu.get_barrier_semaphore()

    def greet_line(i, carry):
        dev = ((here + 1 + (i + 7) % 31) % 32) * 4 + y
        pl.semaphore_signal(barrier, inc=1, device_id=(dev, sa), device_id_type=MESH)
        return carry

    lax.fori_loop(0, 31, greet_line, 0)

    get_index = pltpu.make_async_copy(index_hbm, index_ref, sin.at[0])
    get_chirp = pltpu.make_async_copy(chirp_hbm, chirp_ref, sin.at[1])
    get_chirp.start()
    get_index.start()

    def get_raw(q):
        part = pl.ds(2048 * q, 2048)
        return pltpu.make_async_copy(raw_hbm.at[:, :, part], raw_ref.at[:, :, part], sraw.at[q])

    for q in range(4):
        get_raw(q).start()


    @pl.when(sa != 0)
    def _():
        def greet_source(i, carry):
            dev = (across * 16 + z) * 4 + i
            pl.semaphore_signal(barrier, inc=1, device_id=(dev, xhi), device_id_type=MESH)
            return carry

        lax.fori_loop(0, 4, greet_source, 0)

    def greet_plane(i, carry):
        dev = ((i // 3) * 16 + z) * 4 + (y + 1 + i % 3) % 4
        pl.semaphore_signal(barrier, inc=1, device_id=(dev, sa), device_id_type=MESH)
        return carry

    lax.fori_loop(0, 6, greet_plane, 0)

    @pl.when(sa < 2)
    def _():
        pl.semaphore_signal(barrier, inc=1, device_id=(pa, sa + 1), device_id_type=MESH)

    start = start_ref[0]
    bits = [jnp.bitwise_and(lax.shift_right_logical(start, bit), 1) == 1 for bit in range(11)]

    def shifted(value):
        for bit in (10, 9, 8, 7):
            step = 1 << bit
            value = jnp.where(bits[bit], value[:, step:], value[:, : value.shape[1] - step])
        return value

    get_chirp.wait()

    @pl.when(is_source)
    def _():
        for part in range(2):
            row = jnp.concatenate([chirp_ref[part : part + 1, :].astype(F32), jnp.zeros((1, 256), F32)], axis=1)
            row = jnp.broadcast_to(row, (8, 1280))
            for bit in range(7):
                row = jnp.where(bits[bit], pltpu.roll(row, 1 << bit, 1), row)
            wide = pltpu.roll(jnp.broadcast_to(row[:1], (128, 1280)), 0, 1, stride=1, stride_axis=0)
            wide = wide.astype(BF16)
            for dest in range(4):
                for g in range(4):
                    r0 = part * 128 + g * 32
                    if g > 0:
                        taps_ref[dest, r0 : r0 + 32, : 128 * g] = jnp.zeros((32, 128 * g), BF16)
                    taps_ref[dest, r0 : r0 + 32, 128 * g : 128 * g + 1280] = wide[32 * dest : 32 * dest + 32, :]
                    if g < 3:
                        taps_ref[dest, r0 : r0 + 32, 128 * g + 1280 :] = jnp.zeros((32, 384 - 128 * g), BF16)

    get_index.wait()
    entry = lax.broadcasted_iota(jnp.int32, (32, 128), 0)
    code = jnp.full((32, 128), -2, jnp.int32)
    for dest in range(16):
        index = index_ref[sa, xlo * 64 + 4 * dest + y]
        slot = (index // 512) * 32 + index % 32
        code = jnp.where(entry // 2 == dest, jnp.where((index // 32) % 16 == z, 2 * slot, -2), code)
    pick_ref[...] = (lax.broadcasted_iota(jnp.int32, (32, 128), 1) == code + entry % 2).astype(F32).astype(BF16)

    source_row = lax.broadcasted_iota(jnp.int32, (64, 64), 1)
    target_row = lax.broadcasted_iota(jnp.int32, (64, 64), 0)
    apart = (source_row == 2 * (target_row % 32) + target_row // 32).astype(F32).astype(BF16)
    for q in range(4):
        get_raw(q).wait()
        rows = raw_ref[:, :, 2048 * q : 2048 * q + 2048].reshape(64, 2048)
        rows = jnp.dot(apart, rows, preferred_element_type=F32).astype(BF16)
        planar_ref[0, :, 2048 * q : 2048 * q + 2048] = rows[:32]
        planar_ref[1, :, 2048 * q : 2048 * q + 2048] = rows[32:]

    @pl.when(jnp.logical_or(sa == 1, sa == 2))
    def _():
        for c in range(2):
            for r0 in (0, 16):
                head = jnp.concatenate([jnp.zeros((16, 1920), BF16), planar_ref[c, r0 : r0 + 16, :HALO]], axis=1)
                halo_ref[c, r0 : r0 + 16, :] = shifted(head)

    def correlate(window, jj, t):
        first = (z // 4 + t + 1) % 2
        pieces = []
        for c in range(2):
            for kk in range(2):
                for x in range(2):
                    off = pl.multiple_of(x * 2048 + (first + 2 * kk) * 512, 128)
                    pieces.append(window[c, :, pl.ds(off, SPAN)])
        lhs = jnp.concatenate(pieces, axis=0)
        for dest in range(4):
            got = lax.dot_general(lhs, taps_ref[dest], NT, preferred_element_type=F32)
            real = (got[:128, :128] + got[128:, 128:]).astype(BF16)
            imag = (got[128:, :128] - got[:128, 128:]).astype(BF16)
            for kk in range(2):
                slot = (jj * 4 + first + 2 * kk) * 4 + dest
                for x in range(2):
                    r0 = 64 * kk + 32 * x
                    yb[slot, x, 0] = real[r0 : r0 + 32]
                    yb[slot, x, 1] = imag[r0 : r0 + 32]

    def send_first(jj, t):
        first = (z // 4 + t + 1) % 2

        def send(i, carry):
            k, dest = first + 2 * (i // 4), (y + i) % 4
            dev = ((jnp.where(core == 0, xlo, 1 - xlo)) * 16 + z) * 4 + dest
            target = 2 * core + jj
            there = jnp.logical_or(dev != pa, target != sa)
            slot = (jj * 4 + k) * 4 + dest

            @pl.when(there)
            def _():
                pltpu.make_async_remote_copy(
                    yb.at[slot], xr.at[k, y], sx, rx.at[k],
                    device_id=(dev, target), device_id_type=MESH,
                ).start()

            @pl.when(jnp.logical_not(there))
            def _():
                pltpu.make_async_copy(yb.at[slot], xr.at[k, y], rx.at[k]).start()

            return carry

        lax.fori_loop(0, 8, send, 0)

    @pl.when(is_source)
    def _():
        for c in range(2):
            for r0 in (0, 16):
                w0[c, r0 : r0 + 16, :] = shifted(planar_ref[c, r0 : r0 + 16, :7168])

        def first_half(t, carry):
            correlate(w0, 0, t)
            return carry

        lax.fori_loop(0, 2, first_half, 0)
        for c in range(2):
            for r0 in (0, 16):
                tail = jnp.concatenate([planar_ref[c, r0 : r0 + 16, 4096:], jnp.zeros((16, HALO), BF16)], axis=1)
                w1[c, r0 : r0 + 16, :] = shifted(tail)

    @pl.when(sa == 0)
    def _():
        pl.semaphore_wait(barrier, 41)

    @pl.when(sa == 1)
    def _():
        pl.semaphore_wait(barrier, 46)

    @pl.when(sa == 2)
    def _():
        pl.semaphore_wait(barrier, 38)

    @pl.when(sa == 3)
    def _():
        pl.semaphore_wait(barrier, 37)

    @pl.when(jnp.logical_or(sa == 1, sa == 2))
    def _():
        pltpu.make_async_remote_copy(
            halo_ref, hb, sh, rh,
            device_id=(pa, sa - 1), device_id_type=MESH,
        ).start()

    def row_send(i, carry):
        there = (place + i) % 8
        pltpu.make_async_remote_copy(
            refs_ref, ga.at[place], srow, rrow,
            device_id=(((there // 4) * 16 + z) * 4 + there % 4, sa), device_id_type=MESH,
        ).start()
        return carry

    lax.fori_loop(1, 8, row_send, 0)
    pltpu.make_async_copy(refs_ref, ga.at[place], rrow).start()

    eye = (
        lax.broadcasted_iota(jnp.int32, (128, 128), 0) == lax.broadcasted_iota(jnp.int32, (128, 128), 1)
    ).astype(BF16)

    def far_first(t):
        return (z // 4 + jnp.where(t < 2, 1 + 2 * t, 6 - 2 * t)) % 4

    def pass_on(k):
        pltpu.make_async_copy(xr.at[k], xr.at[k], rx.at[k]).wait()
        for x in range(2):
            pulses = jnp.concatenate([xr[k, :, x, c].reshape(128, 128) for c in range(2)], axis=0)
            flipped = lax.dot_general(eye, pulses, NT, preferred_element_type=F32).astype(BF16)
            for g in range(4):
                for c in range(2):
                    zs[16 * x + 4 * k + g, c] = flipped[32 * g : 32 * g + 32, 128 * c : 128 * c + 128]

        def send(i, carry):
            dest = (i // 4) * 16 + 4 * k + i % 4

            @pl.when(dest != here)
            def _():
                pltpu.make_async_remote_copy(
                    zs.at[dest], turned_ref.at[across * 16 + z], sz, rzs,
                    device_id=(dest * 4 + y, sa), device_id_type=MESH,
                ).start()

            @pl.when(dest == here)
            def _():
                pltpu.make_async_copy(zs.at[dest], turned_ref.at[across * 16 + z], rzs).start()

            return carry

        lax.fori_loop(0, 8, send, 0)

    @pl.when(is_source)
    def _():
        send_first(0, 0)
        send_first(0, 1)

        def second_half(t, carry):
            @pl.when(sa == 0)
            def _():
                pass_on(far_first(2 * t))
                pass_on(far_first(2 * t + 1))

            @pl.when(t == 0)
            def _():
                pltpu.make_async_copy(hb, hb, rh).wait()
                w1[:, :, REACH - HALO :] = w1[:, :, REACH - HALO :] + hb[...]

            correlate(w1, 1, t)
            send_first(1, t)
            return carry

        lax.fori_loop(0, 2, second_half, 0)

    def rest(t, carry):
        pass_on(far_first(t))
        return carry

    lax.fori_loop(jnp.where(sa == 0, 2, 0), 2, rest, 0)

    pltpu.make_async_copy(ga, ga, rrow).wait()
    wanted = jnp.dot(pick_ref[...], ga[...].reshape(128, 512), preferred_element_type=F32)
    for dest in range(16):
        rs[dest] = wanted[2 * dest : 2 * dest + 2].astype(BF16)

    def row_pass(i, carry):
        dest = (z + i) % 16
        pltpu.make_async_remote_copy(
            rs.at[dest], rz.at[z], szrow, rzrow,
            device_id=((xlo * 16 + dest) * 4 + y, sa), device_id_type=MESH,
        ).start()
        return carry

    lax.fori_loop(1, 16, row_pass, 0)
    pltpu.make_async_copy(rs.at[z], rz.at[z], rzrow).start()

    lax.fori_loop(jnp.where(sa == 0, 4, 2), 4, rest, 0)

    pltpu.make_async_copy(rz, rz, rzrow).wait()
    row_ref[...] = jnp.sum(rz[...].astype(F32), axis=0)

    pltpu.make_async_copy(turned_ref, turned_ref, rzs).wait()
    pltpu.make_async_copy(zs.at[pl.ds(0, 31)], zs.at[pl.ds(0, 31)], sz).wait()
    pltpu.make_async_copy(rs.at[pl.ds(0, 15)], rs.at[pl.ds(0, 15)], szrow).wait()
    pltpu.make_async_copy(ga.at[pl.ds(0, 7)], ga.at[pl.ds(0, 7)], srow).wait()

    @pl.when(jnp.logical_or(sa == 1, sa == 2))
    def _():
        pltpu.make_async_copy(halo_ref, halo_ref, sh).wait()

    @pl.when(sa == 0)
    def _():
        pltpu.make_async_copy(yb.at[pl.ds(0, 28)], yb.at[pl.ds(0, 28)], sx).wait()

    @pl.when(sa == 1)
    def _():
        pltpu.make_async_copy(yb, yb, sx).wait()


def azimuth_kernel(turned_ref, row_ref, out_ref, lhs, taps, image, sems):
    zeros = jnp.zeros((32, 256), BF16)
    for c in range(2):
        lhs[c, 0] = zeros
        lhs[c, 17] = zeros
        for block in range(16):
            for half in range(2):
                lhs[c, block + 1, :, 128 * half : 128 * half + 128] = turned_ref[2 * block + half, c]
    for part in range(2):
        row = jnp.concatenate([row_ref[part : part + 1, :], jnp.zeros((1, 512), F32)], axis=1)
        wide = pltpu.roll(jnp.broadcast_to(row, (256, 1024)), 0, 1, stride=1, stride_axis=0)
        taps[256 * part : 256 * part + 256, :] = wide[:, :768].astype(BF16)
    copies = []
    for side in range(2):
        got = []
        for c in range(2):
            total = None
            for o in range(3):
                rows = lhs[c, 8 * side + o : 8 * side + o + 8].reshape(256, 256)
                piece = lax.dot_general(rows, taps[:, 256 * o : 256 * o + 256], NT, preferred_element_type=F32)
                total = piece if total is None else total + piece
            got.append(total)
        real = got[0][:, :256] + got[1][:, 256:]
        imag = got[1][:, :256] - got[0][:, 256:]
        for block in range(8):
            image[side, :, 0, 256 * block : 256 * block + 256] = real[32 * block : 32 * block + 32]
            image[side, :, 1, 256 * block : 256 * block + 256] = imag[32 * block : 32 * block + 32]
        copies.append(
            pltpu.make_async_copy(image.at[side], out_ref.at[:, :, pl.ds(2048 * side, 2048)], sems.at[side])
        )
        copies[-1].start()
    for copy in copies:
        copy.wait()


def params(**more):
    return pltpu.CompilerParams(vmem_limit_bytes=20 << 20, **more)


def on_device(raw_echo, chirp_replica, azimuth_refs, migration_index, window_start):
    large = (migration_index, chirp_replica, raw_echo, azimuth_refs)
    in_hbm = [pltpu.with_memory_space_constraint(value, pltpu.HBM) for value in large]
    dma = pltpu.SemaphoreType.DMA
    turned, row = pl.pallas_call(
        turn_kernel,
        out_shape=(
            jax.ShapeDtypeStruct((32, 2, 32, 128), BF16),
            jax.ShapeDtypeStruct((2, 512), F32),
        ),
        in_specs=[SMEM, HBM, HBM, HBM, HBM],
        out_specs=(ANY, VMEM),
        scratch_shapes=[
            pltpu.VMEM((32, 2, 8192), BF16),
            pltpu.VMEM((2, 32, 8192), BF16),
            pltpu.SMEM((4, 128), jnp.int32),
            pltpu.VMEM((2, 1024), BF16),
            pltpu.VMEM((4, 256, SPAN), BF16),
            pltpu.VMEM((32, 128), BF16),
            pltpu.VMEM((2, 32, REACH), BF16),
            pltpu.VMEM((2, 32, REACH), BF16),
            pltpu.VMEM((2, 32, HALO), BF16),
            pltpu.VMEM((2, 32, HALO), BF16),
            pltpu.VMEM((32, 2, 2, 32, 128), BF16),
            pltpu.VMEM((4, 4, 2, 2, 32, 128), BF16),
            pltpu.VMEM((32, 2, 32, 128), BF16),
            pltpu.VMEM((8, 8, 2, 512), BF16),
            pltpu.VMEM((16, 2, 512), BF16),
            pltpu.VMEM((16, 2, 512), BF16),
            dma((4,)), dma((2,)), dma, dma, dma, dma((4,)), dma, dma, dma, dma, dma, dma,
        ],
        compiler_params=params(collective_id=0, has_side_effects=True),
        name="corner_turn",
    )(window_start, *in_hbm)

    image = pl.pallas_call(
        azimuth_kernel,
        out_shape=jax.ShapeDtypeStruct((32, 2, 4096), F32),
        in_specs=[VMEM, VMEM],
        out_specs=HBM,
        scratch_shapes=[
            pltpu.VMEM((2, 18, 32, 256), BF16),
            pltpu.VMEM((512, 768), BF16),
            pltpu.VMEM((2, 32, 2, 2048), F32),
            dma((2,)),
        ],
        compiler_params=params(),
        name="azimuth_correlate",
    )(turned, row)
    return image[None]


def solution(mesh):
    placed = (P("pa", None, "sa"), P(), P("pa", None, None), P(), P())
    return jax.shard_map(
        on_device, mesh=mesh, in_specs=placed, out_specs=P("sa", "pa", None, None), check_vma=False
    )
```
